32 devices in a mesh: row: 8 (over y, x, core), col: 4 (over z).
Axes of the slice: x: 2, y: 2, z: 4, core: 2. Of those that a mesh axis runs over, the one named last changes fastest.
Arguments:
- mode_block: float32 [32768, 256], P(('row', 'col')), may hold values from -80 to 80
- k_blocks: float32 [256, 3, 128, 128], P(('row', 'col')), may hold values from -1 to 9
- block_cols: int32 [256, 3], P(('row', 'col')), may hold values from 0 to 255, as said below
- panel_node: int32 [4096], replicated, may hold values from 0 to 32767, as said below
- added_mass: bfloat16 [4096, 4096], P('row', 'col'), may hold values from -0.125 to 0.125
- low_edge: int32 [256], replicated, may hold values from 4 to 8
- high_edge: int32 [256], replicated, may hold values from 40 to 56
Outputs:
- filtered: float32 [32768, 256], P(('row', 'col'))
The draws below stay inside these ranges and needn't reach their ends.
Inputs may be any that keep to these rules, and one draw needn't show every extreme that they name: `panel_node`: distinct shell rows. Cut the panels into 32 aligned blocks of 128; in each block at most 8 panels lie on the 1024 rows of one shell device (rows d * 1024 to (d + 1) * 1024 - 1), exactly 8 for some device, and the panels of a block on one device are consecutive. `block_cols`: row i holds i first, then two different block rows among i - 2 to i + 2 other than i.
All inputs are finite; a program needn't handle non-finite values.
Results may differ from the reference program's by a relative error of at most 0.0015.
Values may be sent and summed in bfloat16 or wider, within the bound.
A program may use at most 64 MiB of HBM per device.

```python
import jax
import jax.numpy as jnp
from jax import lax

NB = 256
BLK = 128
KB = 3
DEGREE = 3
OUTER = 2
ROWS_DEV = 1024
PB = 128
NS = 32768
NP = 4096
DEVICES = 32


def wet_layout(key):
    hull_key, swap_key, spot_key, perm_key = jax.random.split(key, 4)
    spread = (PB + DEVICES - 1) // DEVICES
    capacity = 2 * spread
    heavy_count = max(1, PB // (4 * spread))
    boundary = heavy_count * capacity
    within = jnp.arange(PB)
    position = jnp.where(within < boundary, within // capacity, heavy_count + (within - boundary) // spread)
    offset = jnp.where(within < boundary, within % capacity, (within - boundary) % spread)
    hull_order = jax.random.permutation(hull_key, DEVICES)
    device_order = jnp.tile(hull_order[None, :], (DEVICES, 1))
    heavy_spot = jax.random.randint(swap_key, (DEVICES,), 0, heavy_count)
    second = jax.random.randint(spot_key, (DEVICES,), 0, DEVICES)
    blocks = jnp.arange(DEVICES)
    heavy_value = device_order[blocks, heavy_spot]
    second_value = device_order[blocks, second]
    device_order = device_order.at[blocks, heavy_spot].set(second_value)
    device_order = device_order.at[blocks, second].set(heavy_value)
    source = device_order[:, position]
    counts = jnp.sum((source[:, :, None] == jnp.arange(DEVICES)[None, None, :]).astype(jnp.int32), axis=1)
    before = jnp.cumsum(counts, axis=0) - counts
    base_rank = jnp.take_along_axis(before, source, axis=1)
    rank_on_device = base_rank + offset[None, :]
    row_perms = jax.vmap(lambda sub_key: jax.random.permutation(sub_key, ROWS_DEV))(jax.random.split(perm_key, DEVICES))
    row_pick = row_perms[source, rank_on_device]
    return (source * ROWS_DEV + row_pick).reshape(-1).astype(jnp.int32)


def draw_panel_node(key, part):
    return wet_layout(jax.random.fold_in(key, 7))


def draw_block_cols(key, part):
    block_total = NS // BLK
    index_rows = jnp.arange(block_total)
    offsets = jnp.array([-2, -1, 1, 2], dtype=jnp.int32)
    candidate = index_rows[:, None] + offsets[None, :]
    valid = (candidate >= 0) & (candidate < block_total)
    scores = jax.random.randint(key, (block_total, 4), 0, 1000) * 4 + jnp.arange(4)[None, :]
    scores = jnp.where(valid, scores, 100000)
    top_values, picked = lax.top_k(-scores, 2)
    chosen = jnp.take_along_axis(candidate, picked, axis=1)
    return jnp.concatenate([index_rows[:, None], chosen], axis=1).astype(jnp.int32)


def draw_k_blocks(key, part):
    noise_key, diag_key = jax.random.split(key, 2)
    block_shape = (NS // BLK, KB, BLK, BLK)
    values = jnp.clip(jax.random.normal(noise_key, block_shape, jnp.float32), -6.0, 6.0)
    values = values * (KB * BLK) ** (-0.5)
    diagonal = jnp.exp(jax.random.uniform(diag_key, (NS // BLK, BLK), jnp.float32, jnp.log(2.0), jnp.log(8.0)))
    identity = jnp.eye(BLK, dtype=jnp.float32)
    return values.at[:, 0].add(diagonal[:, :, None] * identity[None, :, :])


def draw_mode_block(key, part):
    base_key, row_key, col_key = jax.random.split(key, 3)
    base = jnp.clip(jax.random.normal(base_key, (NS, NB), jnp.float32), -6.0, 6.0)
    ramp = jnp.exp(jnp.log(3.0) * jnp.arange(NS).astype(jnp.float32) / NS)[:, None]
    row_scale = jnp.exp(jax.random.uniform(row_key, (NS, 1), jnp.float32, 0.0, jnp.log(10.0))) * ramp
    col_scale = jnp.exp(jax.random.uniform(col_key, (1, NB), jnp.float32, 0.0, jnp.log(10.0)))
    return base * row_scale * col_scale / 30.0


def place_ends(values, key, smallest, largest):
    spot = [jax.random.randint(jax.random.fold_in(key, axis), (), 0, length) for axis, length in enumerate(values.shape)]
    longest = values.shape.index(max(values.shape))
    neighbour = spot[:longest] + [(spot[longest] + 1) % values.shape[longest]] + spot[longest + 1:]
    return values.at[tuple(spot)].set(smallest).at[tuple(neighbour)].set(largest)


def strengthened(result, stream_key, source, target, blocks, factor):
    def block_of(axis_at):
        return (jnp.arange(result.shape[axis_at]) // (result.shape[axis_at] // blocks)).reshape((-1,) + (1,) * (result.ndim - 1 - axis_at))

    one_side = jax.random.permutation(stream_key, blocks)[block_of(target)]
    far = (block_of(target) + blocks // 2) % blocks
    return jnp.where((block_of(source) == one_side) | (block_of(source) == far), factor * result, result)


def level_of(own_key, shape, pieces, least, largest):
    factor_of, own = 1.0, jax.random.fold_in(own_key, 6)
    for dim, blocks in pieces:
        draws = jnp.exp(jax.random.uniform(jax.random.fold_in(own, dim), (blocks,), jnp.float32, least / len(pieces), largest / len(pieces)))
        factor_of = factor_of * jnp.repeat(draws, shape[dim] // blocks).reshape([-1 if axis == dim else 1 for axis in range(len(shape))])
    return factor_of


def bell_draw_with(stream_key, shape, deviation, most, pieces, heavy, kind=jnp.bfloat16):
    values = deviation * jax.random.normal(stream_key, shape, jnp.float32)
    if pieces:
        values = values * level_of(stream_key, shape, pieces, -0.22, 0.18)
    return jnp.clip(strengthened(values, jax.random.fold_in(stream_key, 3), *heavy), -most, most).astype(kind)


def setup_inputs(seed: int = 0) -> dict:
    seeds = jax.random.split(jax.random.key(seed), 8)
    return {
        "mode_block": draw_mode_block(jax.random.fold_in(seeds[7], 71), 0),
        "k_blocks": draw_k_blocks(jax.random.fold_in(seeds[7], 71), 0),
        "block_cols": draw_block_cols(jax.random.fold_in(seeds[7], 71), 0),
        "panel_node": draw_panel_node(jax.random.fold_in(seeds[7], 71), 0),
        "added_mass": bell_draw_with(seeds[4], (NP, NP), NP ** -0.5, 0.125, ((0, 8), (1, 4)), (1, 0, 8, 2.0)),
        "low_edge": place_ends(jax.random.randint(seeds[5], (NB,), 4, 9), jax.random.fold_in(seeds[5], 1), 4, 8).astype(jnp.int32),
        "high_edge": place_ends(jax.random.randint(seeds[6], (NB,), 40, 57), jax.random.fold_in(seeds[6], 1), 40, 56).astype(jnp.int32),
    }


def stiffness(vectors, k_blocks, block_cols):
    row_total = k_blocks.shape[0]
    block_size = k_blocks.shape[2]
    blocked = vectors.reshape(row_total, block_size, vectors.shape[1])

    def one_row(paired):
        values, columns = paired
        chosen = blocked[columns]
        return jnp.einsum('kij,kjn->in', values, chosen, precision=lax.Precision.HIGHEST)
    return lax.map(one_row, (k_blocks, block_cols)).reshape(vectors.shape)

def operate(vectors, k_blocks, block_cols, panel_node, added_mass):
    wetted = vectors[panel_node].astype(jnp.bfloat16)
    pressure = jnp.dot(added_mass, wetted, preferred_element_type=jnp.float32)
    loads = jnp.zeros_like(vectors).at[panel_node].set(pressure)
    return stiffness(vectors, k_blocks, block_cols) + loads

def reference(mode_block, k_blocks, block_cols, panel_node, added_mass, low_edge, high_edge):
    lower = low_edge.astype(jnp.float32) * 0.25
    upper = high_edge.astype(jnp.float32) * 0.25
    centre = 0.5 * (upper + lower)
    radius = 0.5 * (upper - lower)
    current = mode_block
    for outer_no in range(OUTER):
        previous = current
        image = operate(current, k_blocks, block_cols, panel_node, added_mass)
        current = (image - centre * current) / radius
        for degree_no in range(DEGREE - 1):
            image = operate(current, k_blocks, block_cols, panel_node, added_mass)
            following = 2.0 * (image - centre * current) / radius - previous
            previous = current
            current = following
        squares = lax.optimization_barrier(jnp.sum(current * current, axis=0))
        current = current / jnp.sqrt(squares / NS + 1e-06)
    return current
```

```python
import functools

import jax
import jax.numpy as jnp
from jax import lax
from jax.experimental import pallas as pl
from jax.experimental.pallas import tpu as pltpu
from jax.sharding import PartitionSpec as P

DEGREE = 3
OUTER = 2
STEPS = DEGREE * OUTER
SUBLANES = 8
LIMIT = 32767.0
MESH = pl.DeviceIdType.MESH


def dot(left, right):
    return jnp.dot(left, right, preferred_element_type=jnp.float32)


def split(value):
    high = value.astype(jnp.bfloat16)
    low = (value - high.astype(jnp.float32)).astype(jnp.bfloat16)
    return high, low


def encode(value, axis):
    largest = jnp.maximum(jnp.max(jnp.abs(value), axis=axis, keepdims=True), 1e-30)
    coded = jnp.round(value * (LIMIT / largest))
    return coded.astype(jnp.int32).astype(jnp.int16), largest * (1.0 / LIMIT)


def decode(coded, scale):
    return coded.astype(jnp.int32).astype(jnp.float32) * scale


def kernel(
    n_row, n_col,
    cols_ref, panel_ref, low_ref, high_ref, start_ref, k_ref, mass_ref,
    result_ref, scale_ref,
    vb, v_hi, v_lo, stiff, k_in, k_hi, k_lo, mass, rep, pick, place, order_in, order_out,
    first_out, first_in, disp_out, disp_in, disp_s, disp_si, wet,
    rs_out, rs_in, rs_s, rs_si, pressure,
    ret_out, ret_in, ret_s, ret_si, halo_out, halo_in, halo_s, halo_si,
    centre, inverse, norm, sq_out, sq_in,
    load_sem, mass_send, mass_recv, first_send, first_recv, disp_send, disp_recv, wet_send, wet_recv,
    rs_send, rs_recv, ret_send, ret_recv, halo_send, halo_recv, sq_send, sq_recv,
):
    n_dev = n_row * n_col
    my_row = lax.axis_index("row")
    my_col = lax.axis_index("col")
    me = my_row * n_col + my_col
    rows, width = v_hi.shape
    slots = disp_out.shape[1]
    flat = n_dev * slots
    blocks, terms, block = k_in.shape[0], k_in.shape[1], k_in.shape[2]
    pair = 2 * block
    pairs = rows // pair
    per_block = order_in.shape[0]

    def device(index):
        return (index // n_col, lax.rem(index, n_col))

    barrier = pltpu.get_barrier_semaphore()

    def greet(k, carry):
        pl.semaphore_signal(
            barrier, inc=1, device_id=device(lax.rem(me + k, n_dev)), device_id_type=MESH
        )
        return carry

    lax.fori_loop(1, n_dev, greet, 0)

    load_start = pltpu.make_async_copy(start_ref, vb.at[0], load_sem.at[0])
    load_k = pltpu.make_async_copy(k_ref, k_in, load_sem.at[1])
    load_start.start()
    load_k.start()

    def build_tables():
        def repeat(j, carry):
            named = lax.rem(j, n_col) * n_row + j // n_col
            spot = pl.ds(pl.multiple_of(j * slots, slots), slots)
            rep[spot, :] = jnp.broadcast_to(panel_ref[pl.ds(named, 1), :], (slots, per_block))
            return carry

        lax.fori_loop(0, n_dev, repeat, 0)
        cube = (n_dev, slots, per_block)
        slot_of = lax.broadcasted_iota(jnp.int32, cube, 1).reshape(flat, per_block)
        owner_of = lax.broadcasted_iota(jnp.int32, cube, 0).reshape(flat, per_block)
        lane = lax.broadcasted_iota(jnp.int32, (flat, per_block), 1)

        def hits(values, base):
            owned = (values >= base) & (values < base + rows)
            spot = jnp.where(owned, lane, per_block).astype(jnp.float32)
            first = jnp.min(spot, axis=1, keepdims=True).astype(jnp.int32)
            return owned & (lane - first == slot_of)

        values = rep[...]
        hit = hits(values, me * rows)
        local = jnp.where(hit, values - me * rows + 1, 0).astype(jnp.float32)
        local = jnp.sum(local, axis=1, keepdims=True) - 1.0
        across = jnp.broadcast_to(local, (flat, per_block)).T[0:1, :].astype(jnp.int32)
        down = local.astype(jnp.int32)
        one = jnp.ones((), jnp.float32)
        zero = jnp.zeros((), jnp.float32)
        wide = lax.broadcasted_iota(jnp.int32, (flat, rows), 1)
        pick[...] = jnp.where(wide == down, one, zero).astype(jnp.bfloat16)
        tall = lax.broadcasted_iota(jnp.int32, (rows, flat), 0)
        place[...] = jnp.where(tall == across, one, zero).astype(jnp.bfloat16)
        mine = jnp.broadcast_to(
            panel_ref[pl.ds(my_col * n_row + my_row, 1), :], (flat, per_block)
        )
        order = jnp.where(hits(mine, owner_of * rows), one, zero)
        order_out[...] = order.astype(jnp.bfloat16)
        order_in[...] = order.T.astype(jnp.bfloat16)

    lower = low_ref[...].astype(jnp.float32) * 0.25
    upper = high_ref[...].astype(jnp.float32) * 0.25
    centre[...] = 0.5 * (upper + lower)
    inverse[...] = 1.0 / (0.5 * (upper - lower))
    norm[...] = jnp.ones_like(norm)
    build_tables()
    pl.semaphore_wait(barrier, n_dev - 1)

    def remote(source, target, send, recv, to):
        return pltpu.make_async_remote_copy(
            src_ref=source, dst_ref=target, send_sem=send, recv_sem=recv,
            device_id=to, device_id_type=MESH,
        )

    def everyone(act):
        def step(k, carry):
            act(k, lax.rem(me + k, n_dev))
            return carry

        lax.fori_loop(1, n_dev, step, 0)

    def sum_copy(outer, k, to):
        return remote(sq_out, sq_in.at[outer, me], sq_send.at[k], sq_recv.at[k], device(to))

    def first_copy(k, to):
        return remote(
            first_out.at[to], first_in.at[me], first_send.at[k], first_recv.at[k], device(to)
        )

    def coded_copies(out, out_s, into, into_s, send, recv, slot, k, to):
        where = device(to)
        return (
            remote(out.at[to], into.at[slot, me], send.at[0, k], recv.at[slot, 0, k], where),
            remote(out_s.at[to], into_s.at[slot, me], send.at[1, k], recv.at[slot, 1, k], where),
        )

    disp_copies = functools.partial(
        coded_copies, disp_out, disp_s, disp_in, disp_si, disp_send, disp_recv
    )
    ret_copies = functools.partial(
        coded_copies, ret_out, ret_s, ret_in, ret_si, ret_send, ret_recv
    )

    def exchange_start(copies, slot):
        def act(k, to):
            for copy in copies(slot, k, to):
                copy.start()

        everyone(act)

    def exchange_wait(copies, slot):
        def act(k, to):
            for copy in copies(slot, k, to):
                copy.wait()

        everyone(act)

    def scatter_coded(value, out, out_s, into, into_s, copies, slot):
        coded, scale = encode(value.reshape(n_dev, slots, width), 1)
        out[...] = coded
        out_s[...] = scale
        exchange_start(copies, slot)
        into[slot, me] = out[me]
        into_s[slot, me] = out_s[me]

    def collect(into, into_s, slot):
        return split(decode(into[slot], into_s[slot]).reshape(flat, width))

    chips = n_row // 2
    partner = my_row + 1 - 2 * lax.rem(my_row, 2)

    def wet_copy(k):
        to = (lax.rem(my_row + 2 * k, n_row), my_col)
        return remote(wet.at[my_row], wet.at[my_row], wet_send.at[k], wet_recv.at[k], to)

    def wet_forward(k):
        held = wet.at[lax.rem(my_row + n_row - 2 * k, n_row)]
        return remote(
            held, held, wet_send.at[chips + k], wet_recv.at[chips + k], (partner, my_col)
        )

    def gather_start():
        for k in range(1, chips):
            wet_copy(k).start()
        wet_forward(0).start()

    def gather_wait():
        for k in range(1, chips):
            wet_copy(k).wait_recv()
            wet_forward(k).start()
        for k in range(1, chips):
            wet_copy(k).wait_send()
        for k in range(chips):
            wet_forward(k).wait()

    def rs_copies(k):
        to = lax.rem(my_col + k, n_col)
        where = (my_row, to)
        return (
            remote(rs_out.at[to], rs_in.at[my_col], rs_send.at[0, k], rs_recv.at[0, k], where),
            remote(rs_s.at[to], rs_si.at[my_col], rs_send.at[1, k], rs_recv.at[1, k], where),
        )

    def product_start():
        gathered = wet[...].reshape(n_row * per_block, width)

        def product(index):
            chunk = pl.ds(pl.multiple_of(index * per_block, per_block), per_block)
            return dot(mass[chunk, :], gathered)

        for k in range(1, n_col):
            other = lax.rem(my_col + k, n_col)
            coded, scale = encode(product(other), 0)
            rs_out[other] = coded
            rs_s[other] = scale
            for copy in rs_copies(k):
                copy.start()
        pressure[...] = product(my_col)

    def product_wait():
        for k in range(1, n_col):
            for copy in rs_copies(k):
                copy.wait()
        total = pressure[...]
        for k in range(1, n_col):
            other = lax.rem(my_col + k, n_col)
            total = total + decode(rs_in[other], rs_si[other])
        pressure[...] = total

    def halo_copies(side):
        where = device(lax.rem(me + (1 if side == 0 else n_dev - 1), n_dev))
        return (
            remote(
                halo_out.at[side], halo_in.at[side], halo_send.at[0, side], halo_recv.at[0, side],
                where,
            ),
            remote(
                halo_s.at[side], halo_si.at[side], halo_send.at[1, side], halo_recv.at[1, side],
                where,
            ),
        )

    def halo_start(slot):
        for side in range(2):
            edge = vb[slot, rows - pair : rows, :] if side == 0 else vb[slot, 0:pair, :]
            coded, scale = encode(edge, 0)
            halo_out[side] = coded
            halo_s[side] = scale
            for copy in halo_copies(side):
                copy.start()

    def banded(q, first, values_hi, values_lo):
        count = values_hi.shape[0]
        window_hi = k_hi[q, :, first : first + count]
        window_lo = k_lo[q, :, first : first + count]
        return (
            dot(window_hi, values_hi) + dot(window_lo, values_hi) + dot(window_hi, values_lo)
        )

    def build_band():
        for q in range(pairs):
            for half in range(2):
                i = 2 * q + half
                base = me * blocks - 2 + 2 * q
                for o in range(6):
                    total = jnp.zeros((block, block), jnp.float32)
                    for k in range(terms):
                        flag = (cols_ref[k, i] - base == o).astype(jnp.float32)
                        total = total + k_in[i, k] * flag
                    high, low = split(total)
                    k_hi[q, half * block : (half + 1) * block, o * block : (o + 1) * block] = high
                    k_lo[q, half * block : (half + 1) * block, o * block : (o + 1) * block] = low

    def inner_stiffness():
        for q in range(pairs):
            first = max(q - 1, 0) * pair
            last = min(q + 2, pairs) * pair
            stiff[q * pair : (q + 1) * pair, :] = banded(
                q, pair if q == 0 else 0, v_hi[first:last, :], v_lo[first:last, :]
            )

    def outer_stiffness():
        for side in range(2):
            for copy in halo_copies(side):
                copy.wait()
        high, low = split(decode(halo_in[0], halo_si[0]))
        stiff[0:pair, :] += banded(0, 0, high, low)
        high, low = split(decode(halo_in[1], halo_si[1]))
        stiff[rows - pair : rows, :] += banded(pairs - 1, 2 * pair, high, low)

    def alpha(step):
        start = lax.rem(step, DEGREE) == 0
        factor = jnp.where(start, 1.0, 2.0).astype(jnp.float32)
        scaled = start & (step > 0)
        return inverse[...] * factor * jnp.where(scaled, norm[...], 1.0)

    def beta(step):
        place_in = lax.rem(step, DEGREE)
        factor = jnp.where(place_in == 0, 0.0, 1.0).astype(jnp.float32)
        scaled = (place_in == 1) & (step > 1)
        return factor * jnp.where(scaled, norm[...], 1.0)

    def known_part(step, slot):
        mine = alpha(step) * (stiff[...] - centre[...] * vb[slot])
        mine = mine - beta(step) * vb[1 - slot]
        stiff[...] = mine

    def send_known(step):
        high, low = split(stiff[...])
        chosen = dot(pick[...], high) + dot(pick[...], low)
        scatter_coded(
            chosen, disp_out, disp_s, disp_in, disp_si, disp_copies, lax.rem(step, 2)
        )

    def send_pressure(slot):
        high, low = split(pressure[...])
        ordered = dot(order_out[...], high) + dot(order_out[...], low)
        scatter_coded(ordered, ret_out, ret_s, ret_in, ret_si, ret_copies, slot)

    def next_values(step, slot):
        parity = lax.rem(step, 2)
        exchange_wait(ret_copies, parity)
        high, low = collect(ret_in, ret_si, parity)
        loads = dot(place[...], high) + dot(place[...], low)
        vb[1 - slot] = stiff[...] + alpha(step) * loads

    def square_start(outer, slot):
        now = vb[slot]
        sq_out[...] = jnp.sum(now * now, axis=0, keepdims=True)
        everyone(lambda k, to: sum_copy(outer, k, to).start())
        sq_in[outer, me] = sq_out[...]

    def square_wait(outer):
        everyone(lambda k, to: sum_copy(outer, k, to).wait())
        squares = jnp.sum(sq_in[outer], axis=0)
        return 1.0 / jnp.sqrt(squares / (rows * n_dev) + 1e-06)

    def split_values(slot):
        high, low = split(vb[slot])
        v_hi[...] = high
        v_lo[...] = low

    def mass_place(i):
        index = n_col * my_row + i
        to = lax.rem(index, n_row)
        source = mass_ref.at[pl.ds(i * per_block, per_block), :]
        spot = pl.multiple_of((index // n_row) * per_block, per_block)
        return to, source, mass.at[pl.ds(spot, per_block), :], index // n_row

    def mass_start():
        for i in range(n_col):
            to, source, target, spot = mass_place(i)

            @pl.when(to != my_row)
            def _():
                remote(source, target, mass_send.at[i], mass_recv.at[spot], (to, my_col)).start()

            @pl.when(to == my_row)
            def _():
                pltpu.make_async_copy(source, target, mass_send.at[i]).start()

    def mass_wait():
        for i in range(n_col):
            to, source, target, spot = mass_place(i)

            @pl.when(to != my_row)
            def _():
                remote(
                    source, target, mass_send.at[i], mass_recv.at[spot], (to, my_col)
                ).wait_send()

            @pl.when(to == my_row)
            def _():
                pltpu.make_async_copy(source, target, mass_send.at[i]).wait()

        for q in range(n_col):
            index = q * n_row + my_row
            target = mass.at[pl.ds(q * per_block, per_block), :]
            source = mass_ref.at[pl.ds(0, per_block), :]

            @pl.when(index // n_col != my_row)
            def _():
                remote(
                    source, target, mass_send.at[q], mass_recv.at[q], (index // n_col, my_col)
                ).wait_recv()

    load_start.wait()
    split_values(0)
    first_out[...] = dot(pick[...], v_hi[...]).reshape(n_dev, slots, width).astype(jnp.bfloat16)
    everyone(lambda k, to: first_copy(k, to).start())
    first_in[me] = first_out[me]
    halo_start(0)
    mass_start()
    load_k.wait()
    build_band()
    inner_stiffness()
    everyone(lambda k, to: first_copy(k, to).wait())
    arrived = first_in[...].astype(jnp.float32).reshape(flat, width).astype(jnp.bfloat16)
    wet[my_row] = dot(order_in[...], arrived).astype(jnp.bfloat16)
    gather_start()
    outer_stiffness()
    gather_wait()
    mass_wait()
    product_start()
    known_part(0, 0)
    send_known(0)
    product_wait()

    def step_of(step, carry):
        slot = lax.rem(step, 2)
        send_pressure(slot)
        exchange_wait(disp_copies, slot)
        high, low = collect(disp_in, disp_si, slot)
        known = dot(order_in[...], high) + dot(order_in[...], low)
        wet[my_row] = (known + alpha(step) * pressure[...]).astype(jnp.bfloat16)
        gather_start()
        next_values(step, slot)
        halo_start(1 - slot)
        ends = lax.rem(step, DEGREE) == DEGREE - 1
        outer = step // DEGREE

        @pl.when(ends)
        def _():
            square_start(outer, 1 - slot)

        split_values(1 - slot)
        gather_wait()
        product_start()
        inner_stiffness()
        outer_stiffness()

        @pl.when(ends)
        def _():
            norm[...] = square_wait(outer)

        known_part(step + 1, 1 - slot)

        @pl.when(step < STEPS - 2)
        def _():
            send_known(step + 1)

        product_wait()
        return carry

    lax.fori_loop(0, STEPS - 1, step_of, 0)
    last = STEPS - 1
    slot = last % 2
    send_pressure(slot)
    next_values(last, slot)
    square_start(OUTER - 1, 1 - slot)
    store = pltpu.make_async_copy(vb.at[1 - slot], result_ref, load_sem.at[0])
    store.start()
    scale_ref[...] = square_wait(OUTER - 1)
    store.wait()


def body(mode_block, k_blocks, block_cols, panel_node, added_mass, low_edge, high_edge):
    n_row = lax.axis_size("row")
    n_col = lax.axis_size("col")
    devices = n_row * n_col
    rows_dev, width = mode_block.shape
    block_size = k_blocks.shape[2]
    per_block = panel_node.shape[0] // devices
    most = 2 * ((per_block + devices - 1) // devices)
    slots = (most + SUBLANES - 1) // SUBLANES * SUBLANES
    flat = devices * slots
    pair = 2 * block_size
    pairs = rows_dev // pair
    f32, bf16, i16 = jnp.float32, jnp.bfloat16, jnp.int16
    vmem = pl.BlockSpec(memory_space=pltpu.VMEM)
    anywhere = pl.BlockSpec(memory_space=pl.ANY)
    dma = pltpu.SemaphoreType.DMA
    coded = pltpu.VMEM((devices, slots, width), i16)
    coded_in = pltpu.VMEM((2, devices, slots, width), i16)
    scale = pltpu.VMEM((devices, 1, width), f32)
    scale_in = pltpu.VMEM((2, devices, 1, width), f32)
    row = pltpu.VMEM((1, width), f32)
    values, factor = pl.pallas_call(
        functools.partial(kernel, n_row, n_col),
        out_shape=(
            jax.ShapeDtypeStruct(mode_block.shape, f32),
            jax.ShapeDtypeStruct((1, width), f32),
        ),
        in_specs=[pl.BlockSpec(memory_space=pltpu.SMEM), vmem, vmem, vmem]
        + [anywhere] * 3,
        out_specs=(anywhere, vmem),
        scratch_shapes=[
            pltpu.VMEM((2, rows_dev, width), f32),
            pltpu.VMEM((rows_dev, width), bf16),
            pltpu.VMEM((rows_dev, width), bf16),
            pltpu.VMEM((rows_dev, width), f32),
            pltpu.VMEM(k_blocks.shape, f32),
            pltpu.VMEM((pairs, pair, 3 * pair), bf16),
            pltpu.VMEM((pairs, pair, 3 * pair), bf16),
            pltpu.VMEM(added_mass.shape, bf16),
            pltpu.VMEM((flat, per_block), jnp.int32),
            pltpu.VMEM((flat, rows_dev), bf16),
            pltpu.VMEM((rows_dev, flat), bf16),
            pltpu.VMEM((per_block, flat), bf16),
            pltpu.VMEM((flat, per_block), bf16),
            pltpu.VMEM((devices, slots, width), bf16),
            pltpu.VMEM((devices, slots, width), bf16),
            coded, coded_in, scale, scale_in,
            pltpu.VMEM((n_row, per_block, width), bf16),
            pltpu.VMEM((n_col, per_block, width), i16),
            pltpu.VMEM((n_col, per_block, width), i16),
            pltpu.VMEM((n_col, 1, width), f32),
            pltpu.VMEM((n_col, 1, width), f32),
            pltpu.VMEM((per_block, width), f32),
            coded, coded_in, scale, scale_in,
            pltpu.VMEM((2, pair, width), i16),
            pltpu.VMEM((2, pair, width), i16),
            pltpu.VMEM((2, 1, width), f32),
            pltpu.VMEM((2, 1, width), f32),
            row, row, row, row,
            pltpu.VMEM((OUTER, devices, 1, width), f32),
            dma((2,)),
            dma((n_col,)),
            dma((n_col,)),
            dma((devices,)),
            dma((devices,)),
            dma((2, devices)),
            dma((2, 2, devices)),
            dma((n_row,)),
            dma((n_row,)),
            dma((2, n_col)),
            dma((2, n_col)),
            dma((2, devices)),
            dma((2, 2, devices)),
            dma((2, 2)),
            dma((2, 2)),
            dma((devices,)),
            dma((devices,)),
        ],
        compiler_params=pltpu.CompilerParams(
            collective_id=0, has_side_effects=True, vmem_limit_bytes=60 * 1024 * 1024
        ),
    )(
        block_cols.T,
        panel_node.reshape(devices, per_block),
        low_edge.reshape(1, width),
        high_edge.reshape(1, width),
        mode_block,
        k_blocks,
        added_mass,
    )
    return values * factor


def solution(mesh):
    placed = (
        P(("row", "col"), None),
        P(("row", "col"), None, None, None),
        P(("row", "col"), None),
        P(),
        P("row", "col"),
        P(),
        P(),
    )
    return jax.shard_map(
        body, mesh=mesh, in_specs=placed, out_specs=P(("row", "col"), None), check_vma=False
    )
```

```python
import functools

import jax
import jax.numpy as jnp
from jax import lax
from jax.experimental import pallas as pl
from jax.experimental.pallas import tpu as pltpu
from jax.sharding import PartitionSpec as P

DEGREE = 3
OUTER = 2
STEPS = DEGREE * OUTER
SUBLANES = 8
LIMIT = 32767.0
MESH = pl.DeviceIdType.MESH


def dot(left, right):
    return jnp.dot(left, right, preferred_element_type=jnp.float32)


def split(value):
    high = value.astype(jnp.bfloat16)
    low = (value - high.astype(jnp.float32)).astype(jnp.bfloat16)
    return high, low


def encode(value, axis):
    largest = jnp.maximum(jnp.max(jnp.abs(value), axis=axis, keepdims=True), 1e-30)
    coded = jnp.round(value * (LIMIT / largest))
    return coded.astype(jnp.int32).astype(jnp.int16), largest * (1.0 / LIMIT)


def decode(coded, scale):
    return coded.astype(jnp.int32).astype(jnp.float32) * scale


def kernel(
    n_row, n_col,
    cols_hbm, panel_hbm, low_hbm, high_hbm, start_ref, k_ref, mass_hbm,
    result_ref, scale_ref,
    cols_ref, panel_ref, low_ref, high_ref, mass_ref, vb, v_hi, v_lo, stiff, k_in, k_hi, k_lo, mass, rep, pick, place, order_in, order_out,
    first_out, first_in, disp_out, disp_in, disp_s, disp_si, wet,
    rs_out, rs_in, rs_s, rs_si, pressure,
    ret_out, ret_in, ret_s, ret_si, halo_out, halo_in, halo_s, halo_si,
    centre, inverse, norm, sq_out, sq_in, dry,
    load_sem, mass_send, mass_recv, first_send, first_recv, disp_send, disp_recv, wet_send, wet_recv,
    rs_send, rs_recv, ret_send, ret_recv, halo_send, halo_recv, sq_send, sq_recv,
):
    n_dev = n_row * n_col
    my_row = lax.axis_index("row")
    my_col = lax.axis_index("col")
    me = my_row * n_col + my_col
    rows, width = v_hi.shape
    slots = disp_out.shape[1]
    flat = n_dev * slots
    blocks, terms, block = k_in.shape[0], k_in.shape[1], k_in.shape[2]
    pair = 2 * block
    pairs = rows // pair
    per_block = order_in.shape[0]

    def device(index):
        return (index // n_col, lax.rem(index, n_col))

    barrier = pltpu.get_barrier_semaphore()

    def greet(k, carry):
        pl.semaphore_signal(
            barrier, inc=1, device_id=device(lax.rem(me + k, n_dev)), device_id_type=MESH
        )
        return carry

    lax.fori_loop(1, n_dev, greet, 0)

    load_start = pltpu.make_async_copy(start_ref, vb.at[0], load_sem.at[0])
    load_k = pltpu.make_async_copy(k_ref, k_in, load_sem.at[1])
    load_mass = pltpu.make_async_copy(mass_hbm, mass_ref, load_sem.at[2])
    load_small = [
        pltpu.make_async_copy(source, target, load_sem.at[3 + i])
        for i, (source, target) in enumerate(
            ((panel_hbm, panel_ref), (low_hbm, low_ref), (high_hbm, high_ref), (cols_hbm, cols_ref))
        )
    ]
    for load in load_small:
        load.start()
    load_start.start()
    load_mass.start()
    load_k.start()
    for load in load_small:
        load.wait()

    def build_tables():
        def repeat(j, carry):
            named = lax.rem(j, n_col) * n_row + j // n_col
            spot = pl.ds(pl.multiple_of(j * slots, slots), slots)
            rep[spot, :] = jnp.broadcast_to(panel_ref[pl.ds(named, 1), :], (slots, per_block))
            return carry

        lax.fori_loop(0, n_dev, repeat, 0)
        cube = (n_dev, slots, per_block)
        slot_of = lax.broadcasted_iota(jnp.int32, cube, 1).reshape(flat, per_block)
        owner_of = lax.broadcasted_iota(jnp.int32, cube, 0).reshape(flat, per_block)
        lane = lax.broadcasted_iota(jnp.int32, (flat, per_block), 1)

        def hits(values, base):
            owned = (values >= base) & (values < base + rows)
            spot = jnp.where(owned, lane, per_block).astype(jnp.float32)
            first = jnp.min(spot, axis=1, keepdims=True).astype(jnp.int32)
            return owned & (lane - first == slot_of)

        values = rep[...]
        hit = hits(values, me * rows)
        local = jnp.where(hit, values - me * rows + 1, 0).astype(jnp.float32)
        local = jnp.sum(local, axis=1, keepdims=True) - 1.0
        across = jnp.broadcast_to(local, (flat, per_block)).T[0:1, :].astype(jnp.int32)
        down = local.astype(jnp.int32)
        one = jnp.ones((), jnp.float32)
        zero = jnp.zeros((), jnp.float32)
        wide = lax.broadcasted_iota(jnp.int32, (flat, rows), 1)
        pick[...] = jnp.where(wide == down, one, zero).astype(jnp.bfloat16)
        tall = lax.broadcasted_iota(jnp.int32, (rows, flat), 0)
        place[...] = jnp.where(tall == across, one, zero).astype(jnp.bfloat16)
        mine = jnp.broadcast_to(
            panel_ref[pl.ds(my_col * n_row + my_row, 1), :], (flat, per_block)
        )
        order = jnp.where(hits(mine, owner_of * rows), one, zero)
        order_out[...] = order.astype(jnp.bfloat16)
        order_in[...] = order.T.astype(jnp.bfloat16)

    lower = low_ref[...].astype(jnp.float32) * 0.25
    upper = high_ref[...].astype(jnp.float32) * 0.25
    centre[...] = 0.5 * (upper + lower)
    inverse[...] = 1.0 / (0.5 * (upper - lower))
    norm[...] = jnp.ones_like(norm)
    build_tables()
    pl.semaphore_wait(barrier, n_dev - 1)

    def remote(source, target, send, recv, to):
        return pltpu.make_async_remote_copy(
            src_ref=source, dst_ref=target, send_sem=send, recv_sem=recv,
            device_id=to, device_id_type=MESH,
        )

    def everyone(act):
        def line(k, first):
            row = lax.rem(my_row + k, n_row)
            for j in range(first, n_col):
                col = lax.rem(my_col + j, n_col)
                act(row * n_col + col, (row, col))

        line(0, 1)

        def step(k, carry):
            line(k, 0)
            return carry

        lax.fori_loop(1, n_row, step, 0)

    partner = my_row + 1 - 2 * lax.rem(my_row, 2)

    def wait_everyone(out, into, send, recv):
        others = pl.ds(0, n_dev - 1)
        remote(out.at[others], into.at[others], send, recv, (partner, my_col)).wait()

    def first_copy(to, where):
        return remote(first_out.at[to], first_in.at[me], first_send.at[0], first_recv.at[0], where)

    def coded_copies(out, out_s, into, into_s, send, recv, slot, to, where):
        return (
            remote(out.at[to], into.at[slot, me], send.at[0], recv.at[slot, 0], where),
            remote(out_s.at[to], into_s.at[slot, me], send.at[1], recv.at[slot, 1], where),
        )

    disp_copies = functools.partial(
        coded_copies, disp_out, disp_s, disp_in, disp_si, disp_send, disp_recv
    )
    ret_copies = functools.partial(
        coded_copies, ret_out, ret_s, ret_in, ret_si, ret_send, ret_recv
    )

    def exchange_start(copies, slot):
        def act(to, where):
            for copy in copies(slot, to, where):
                copy.start()

        everyone(act)

    def disp_wait(slot):
        wait_everyone(disp_out, disp_in.at[slot], disp_send.at[0], disp_recv.at[slot, 0])
        wait_everyone(disp_s, disp_si.at[slot], disp_send.at[1], disp_recv.at[slot, 1])

    def ret_wait(slot):
        wait_everyone(ret_out, ret_in.at[slot], ret_send.at[0], ret_recv.at[slot, 0])
        wait_everyone(ret_s, ret_si.at[slot], ret_send.at[1], ret_recv.at[slot, 1])

    def scatter_coded(value, out, out_s, into, into_s, copies, slot):
        coded, scale = encode(value.reshape(n_dev, slots, width), 1)
        out[...] = coded
        out_s[...] = scale
        exchange_start(copies, slot)
        into[slot, me] = out[me]
        into_s[slot, me] = out_s[me]

    def collect(into, into_s, slot):
        return split(decode(into[slot], into_s[slot]).reshape(flat, width))

    chips = n_row // 2

    def wet_copy(k):
        to = (lax.rem(my_row + 2 * k, n_row), my_col)
        return remote(wet.at[my_row], wet.at[my_row], wet_send.at[k], wet_recv.at[k], to)

    def wet_forward(k):
        held = wet.at[lax.rem(my_row + n_row - 2 * k, n_row)]
        return remote(
            held, held, wet_send.at[chips + k], wet_recv.at[chips + k], (partner, my_col)
        )

    def gather_start():
        for k in range(1, chips):
            wet_copy(k).start()
        wet_forward(0).start()

    def gather_wait():
        for k in range(1, chips):
            wet_copy(k).wait_recv()
            wet_forward(k).start()
        for k in range(1, chips):
            wet_copy(k).wait_send()
        for k in range(chips):
            wet_forward(k).wait()

    def rs_copies(k):
        to = lax.rem(my_col + k, n_col)
        where = (my_row, to)
        return (
            remote(rs_out.at[to], rs_in.at[my_col], rs_send.at[0], rs_recv.at[0], where),
            remote(rs_s.at[to], rs_si.at[my_col], rs_send.at[1], rs_recv.at[1], where),
        )

    def product_start():
        gathered = wet[...].reshape(n_row * per_block, width)

        def product(index):
            chunk = pl.ds(pl.multiple_of(index * per_block, per_block), per_block)
            return dot(mass[chunk, :], gathered)

        for k in range(1, n_col):
            other = lax.rem(my_col + k, n_col)
            coded, scale = encode(product(other), 0)
            rs_out[other] = coded
            rs_s[other] = scale
            for copy in rs_copies(k):
                copy.start()
        pressure[...] = product(my_col)

    def product_wait():
        others = pl.ds(0, n_col - 1)
        where = (partner, my_col)
        remote(rs_out.at[others], rs_in.at[others], rs_send.at[0], rs_recv.at[0], where).wait()
        remote(rs_s.at[others], rs_si.at[others], rs_send.at[1], rs_recv.at[1], where).wait()
        total = pressure[...]
        for k in range(1, n_col):
            other = lax.rem(my_col + k, n_col)
            total = total + decode(rs_in[other], rs_si[other])
        pressure[...] = total

    def halo_copies(side):
        where = device(lax.rem(me + (1 if side == 0 else n_dev - 1), n_dev))
        return (
            remote(
                halo_out.at[side], halo_in.at[side], halo_send.at[0, side], halo_recv.at[0, side],
                where,
            ),
            remote(
                halo_s.at[side], halo_si.at[side], halo_send.at[1, side], halo_recv.at[1, side],
                where,
            ),
        )

    def halo_start(slot):
        for side in range(2):
            edge = vb[slot, rows - pair : rows, :] if side == 0 else vb[slot, 0:pair, :]
            coded, scale = encode(edge, 0)
            halo_out[side] = coded
            halo_s[side] = scale
            for copy in halo_copies(side):
                copy.start()

    def banded(q, first, values_hi, values_lo):
        count = values_hi.shape[0]
        window_hi = k_hi[q, :, first : first + count]
        window_lo = k_lo[q, :, first : first + count]
        return (
            dot(window_hi, values_hi) + dot(window_lo, values_hi) + dot(window_hi, values_lo)
        )

    def build_band():
        for q in range(pairs):
            for half in range(2):
                i = 2 * q + half
                base = me * blocks - 2 + 2 * q
                for o in range(6):
                    total = jnp.zeros((block, block), jnp.float32)
                    for k in range(terms):
                        flag = (cols_ref[k, i] - base == o).astype(jnp.float32)
                        total = total + k_in[i, k] * flag
                    high, low = split(total)
                    k_hi[q, half * block : (half + 1) * block, o * block : (o + 1) * block] = high
                    k_lo[q, half * block : (half + 1) * block, o * block : (o + 1) * block] = low

    def inner_stiffness():
        for q in range(pairs):
            first = max(q - 1, 0) * pair
            last = min(q + 2, pairs) * pair
            stiff[q * pair : (q + 1) * pair, :] = banded(
                q, pair if q == 0 else 0, v_hi[first:last, :], v_lo[first:last, :]
            )

    def outer_stiffness():
        for side in range(2):
            for copy in halo_copies(side):
                copy.wait()
        high, low = split(decode(halo_in[0], halo_si[0]))
        stiff[0:pair, :] += banded(0, 0, high, low)
        high, low = split(decode(halo_in[1], halo_si[1]))
        stiff[rows - pair : rows, :] += banded(pairs - 1, 2 * pair, high, low)

    def alpha(step):
        start = lax.rem(step, DEGREE) == 0
        factor = jnp.where(start, 1.0, 2.0).astype(jnp.float32)
        scaled = start & (step > 0)
        return inverse[...] * factor * jnp.where(scaled, norm[...], 1.0)

    def beta(step):
        place_in = lax.rem(step, DEGREE)
        factor = jnp.where(place_in == 0, 0.0, 1.0).astype(jnp.float32)
        scaled = (place_in == 1) & (step > 1)
        return factor * jnp.where(scaled, norm[...], 1.0)

    def known_part(step, slot):
        mine = alpha(step) * (stiff[...] - centre[...] * vb[slot])
        mine = mine - beta(step) * vb[1 - slot]
        stiff[...] = mine

    def send_known(step):
        high, low = split(stiff[...])
        chosen = dot(pick[...], high) + dot(pick[...], low)
        scatter_coded(
            chosen, disp_out, disp_s, disp_in, disp_si, disp_copies, lax.rem(step, 2)
        )

    def send_pressure(slot):
        high, low = split(pressure[...])
        ordered = dot(order_out[...], high) + dot(order_out[...], low)
        scatter_coded(ordered, ret_out, ret_s, ret_in, ret_si, ret_copies, slot)

    def next_values(step, slot):
        parity = lax.rem(step, 2)
        ret_wait(parity)
        high, low = collect(ret_in, ret_si, parity)
        loads = dot(place[...], high) + dot(place[...], low)
        vb[1 - slot] = stiff[...] + alpha(step) * loads

    def square_start(outer, panels):
        shells = stiff[...] * dry[...]
        sq_out[...] = jnp.sum(shells * shells, axis=0, keepdims=True) + jnp.sum(
            panels * panels, axis=0, keepdims=True
        )

        def act(to, where):
            remote(sq_out, sq_in.at[outer, me], sq_send.at[outer], sq_recv.at[outer], where).start()

        everyone(act)
        sq_in[outer, me] = sq_out[...]

    def square_wait(outer):
        arrived = sq_in.at[outer]
        wait_everyone(arrived, arrived, sq_send.at[outer], sq_recv.at[outer])
        squares = jnp.sum(sq_in[outer], axis=0)
        return 1.0 / jnp.sqrt(squares / (rows * n_dev) + 1e-06)

    def panel_values(step):
        slot = lax.rem(step, 2)
        disp_wait(slot)
        high, low = collect(disp_in, disp_si, slot)
        known = dot(order_in[...], high) + dot(order_in[...], low)
        return known + alpha(step) * pressure[...]

    def split_values(slot):
        high, low = split(vb[slot])
        v_hi[...] = high
        v_lo[...] = low

    def mass_place(i):
        index = n_col * my_row + i
        to = lax.rem(index, n_row)
        source = mass_ref.at[pl.ds(i * per_block, per_block), :]
        spot = pl.multiple_of((index // n_row) * per_block, per_block)
        return to, source, mass.at[pl.ds(spot, per_block), :], index // n_row

    def mass_start():
        for i in range(n_col):
            to, source, target, spot = mass_place(i)

            @pl.when(to != my_row)
            def _():
                remote(source, target, mass_send.at[i], mass_recv.at[spot], (to, my_col)).start()

            @pl.when(to == my_row)
            def _():
                pltpu.make_async_copy(source, target, mass_send.at[i]).start()

    def mass_wait():
        for i in range(n_col):
            to, source, target, spot = mass_place(i)

            @pl.when(to != my_row)
            def _():
                remote(
                    source, target, mass_send.at[i], mass_recv.at[spot], (to, my_col)
                ).wait_send()

            @pl.when(to == my_row)
            def _():
                pltpu.make_async_copy(source, target, mass_send.at[i]).wait()

        for q in range(n_col):
            index = q * n_row + my_row
            target = mass.at[pl.ds(q * per_block, per_block), :]
            source = mass_ref.at[pl.ds(0, per_block), :]

            @pl.when(index // n_col != my_row)
            def _():
                remote(
                    source, target, mass_send.at[q], mass_recv.at[q], (index // n_col, my_col)
                ).wait_recv()

    load_start.wait()
    split_values(0)
    first_out[...] = dot(pick[...], v_hi[...]).reshape(n_dev, slots, width).astype(jnp.bfloat16)
    everyone(lambda to, where: first_copy(to, where).start())
    first_in[me] = first_out[me]
    halo_start(0)
    load_mass.wait()
    mass_start()
    load_k.wait()
    build_band()
    inner_stiffness()
    ones = jnp.ones((flat, width), jnp.bfloat16)
    dry[...] = 1.0 - dot(place[...], ones)
    wait_everyone(first_out, first_in, first_send.at[0], first_recv.at[0])
    arrived = first_in[...].astype(jnp.float32).reshape(flat, width).astype(jnp.bfloat16)
    wet[my_row] = dot(order_in[...], arrived).astype(jnp.bfloat16)
    gather_start()
    outer_stiffness()
    gather_wait()
    mass_wait()
    product_start()
    known_part(0, 0)
    send_known(0)
    product_wait()

    def step_of(step, carry):
        slot = lax.rem(step, 2)
        ends = lax.rem(step, DEGREE) == DEGREE - 1
        outer = step // DEGREE
        send_pressure(slot)
        panels = panel_values(step)
        wet[my_row] = panels.astype(jnp.bfloat16)
        gather_start()

        @pl.when(ends)
        def _():
            square_start(outer, panels)

        next_values(step, slot)
        halo_start(1 - slot)
        split_values(1 - slot)
        gather_wait()
        product_start()
        inner_stiffness()
        outer_stiffness()

        @pl.when(ends)
        def _():
            norm[...] = square_wait(outer)

        known_part(step + 1, 1 - slot)
        send_known(step + 1)
        product_wait()
        return carry

    lax.fori_loop(0, STEPS - 1, step_of, 0)
    last = STEPS - 1
    slot = last % 2
    send_pressure(slot)
    square_start(OUTER - 1, panel_values(last))
    next_values(last, slot)
    store = pltpu.make_async_copy(vb.at[1 - slot], result_ref, load_sem.at[0])
    store.start()
    scale_ref[...] = square_wait(OUTER - 1)
    store.wait()


def body(mode_block, k_blocks, block_cols, panel_node, added_mass, low_edge, high_edge):
    n_row = lax.axis_size("row")
    n_col = lax.axis_size("col")
    devices = n_row * n_col
    rows_dev, width = mode_block.shape
    block_size = k_blocks.shape[2]
    per_block = panel_node.shape[0] // devices
    most = 2 * ((per_block + devices - 1) // devices)
    slots = (most + SUBLANES - 1) // SUBLANES * SUBLANES
    flat = devices * slots
    pair = 2 * block_size
    pairs = rows_dev // pair
    f32, bf16, i16 = jnp.float32, jnp.bfloat16, jnp.int16
    vmem = pl.BlockSpec(memory_space=pltpu.VMEM)
    anywhere = pl.BlockSpec(memory_space=pl.ANY)
    dma = pltpu.SemaphoreType.DMA
    coded = pltpu.VMEM((devices, slots, width), i16)
    coded_in = pltpu.VMEM((2, devices, slots, width), i16)
    scale = pltpu.VMEM((devices, 1, width), f32)
    scale_in = pltpu.VMEM((2, devices, 1, width), f32)
    row = pltpu.VMEM((1, width), f32)
    values, factor = pl.pallas_call(
        functools.partial(kernel, n_row, n_col),
        out_shape=(
            jax.ShapeDtypeStruct(mode_block.shape, f32),
            jax.ShapeDtypeStruct((1, width), f32),
        ),
        in_specs=[anywhere] * 7,
        out_specs=(anywhere, vmem),
        scratch_shapes=[
            pltpu.SMEM(block_cols.shape[::-1], jnp.int32),
            pltpu.VMEM((devices, per_block), jnp.int32),
            pltpu.VMEM((1, width), jnp.int32),
            pltpu.VMEM((1, width), jnp.int32),
            pltpu.VMEM(added_mass.shape, bf16),
            pltpu.VMEM((2, rows_dev, width), f32),
            pltpu.VMEM((rows_dev, width), bf16),
            pltpu.VMEM((rows_dev, width), bf16),
            pltpu.VMEM((rows_dev, width), f32),
            pltpu.VMEM(k_blocks.shape, f32),
            pltpu.VMEM((pairs, pair, 3 * pair), bf16),
            pltpu.VMEM((pairs, pair, 3 * pair), bf16),
            pltpu.VMEM(added_mass.shape, bf16),
            pltpu.VMEM((flat, per_block), jnp.int32),
            pltpu.VMEM((flat, rows_dev), bf16),
            pltpu.VMEM((rows_dev, flat), bf16),
            pltpu.VMEM((per_block, flat), bf16),
            pltpu.VMEM((flat, per_block), bf16),
            pltpu.VMEM((devices, slots, width), bf16),
            pltpu.VMEM((devices, slots, width), bf16),
            coded, coded_in, scale, scale_in,
            pltpu.VMEM((n_row, per_block, width), bf16),
            pltpu.VMEM((n_col, per_block, width), i16),
            pltpu.VMEM((n_col, per_block, width), i16),
            pltpu.VMEM((n_col, 1, width), f32),
            pltpu.VMEM((n_col, 1, width), f32),
            pltpu.VMEM((per_block, width), f32),
            coded, coded_in, scale, scale_in,
            pltpu.VMEM((2, pair, width), i16),
            pltpu.VMEM((2, pair, width), i16),
            pltpu.VMEM((2, 1, width), f32),
            pltpu.VMEM((2, 1, width), f32),
            row, row, row, row,
            pltpu.VMEM((OUTER, devices, 1, width), f32),
            pltpu.VMEM((rows_dev, width), f32),
            dma((7,)),
            dma((n_col,)),
            dma((n_col,)),
            dma((1,)),
            dma((1,)),
            dma((2,)),
            dma((2, 2)),
            dma((n_row,)),
            dma((n_row,)),
            dma((2,)),
            dma((2,)),
            dma((2,)),
            dma((2, 2)),
            dma((2, 2)),
            dma((2, 2)),
            dma((OUTER,)),
            dma((OUTER,)),
        ],
        compiler_params=pltpu.CompilerParams(
            collective_id=0, has_side_effects=True, vmem_limit_bytes=60 * 1024 * 1024
        ),
    )(
        block_cols.T,
        panel_node.reshape(devices, per_block),
        low_edge.reshape(1, width),
        high_edge.reshape(1, width),
        mode_block,
        k_blocks,
        added_mass,
    )
    return values * factor


def solution(mesh):
    placed = (
        P(("row", "col"), None),
        P(("row", "col"), None, None, None),
        P(("row", "col"), None),
        P(),
        P("row", "col"),
        P(),
        P(),
    )
    return jax.shard_map(
        body, mesh=mesh, in_specs=placed, out_specs=P(("row", "col"), None), check_vma=False
    )
```

```python
import functools

import jax
import jax.numpy as jnp
from jax import lax
from jax.experimental import pallas as pl
from jax.experimental.pallas import tpu as pltpu
from jax.sharding import PartitionSpec as P

DEGREE = 3
OUTER = 2
STEPS = DEGREE * OUTER
SUBLANES = 8
LIMIT = 32767.0
MESH = pl.DeviceIdType.MESH


def dot(left, right):
    return jnp.dot(left, right, preferred_element_type=jnp.float32)


def split(value):
    high = value.astype(jnp.bfloat16)
    low = (value - high.astype(jnp.float32)).astype(jnp.bfloat16)
    return high, low


def encode(value, axis):
    largest = jnp.maximum(jnp.max(jnp.abs(value), axis=axis, keepdims=True), 1e-30)
    coded = jnp.round(value * (LIMIT / largest))
    return coded.astype(jnp.int32).astype(jnp.int16), largest * (1.0 / LIMIT)


def decode(coded, scale):
    return coded.astype(jnp.int32).astype(jnp.float32) * scale


def kernel(
    n_row, n_col,
    cols_hbm, panel_hbm, low_hbm, high_hbm, start_ref, k_ref, mass_hbm,
    result_ref, scale_ref,
    cols_ref, panel_ref, low_ref, high_ref, mass_ref, vb, v_hi, v_lo, stiff, k_in, k_hi, k_lo, mass, rep, pick, place, order_in, order_out,
    first_out, first_in, disp_out, disp_in, disp_s, disp_si, wet,
    rs_out, rs_in, rs_s, rs_si, pressure,
    ret_out, ret_in, ret_s, ret_si, halo_out, halo_in, halo_s, halo_si,
    centre, inverse, norm, sq_out, sq_in, dry,
    load_sem, mass_send, mass_recv, first_send, first_recv, disp_send, disp_recv, wet_send, wet_recv,
    rs_send, rs_recv, ret_send, ret_recv, halo_send, halo_recv, sq_send, sq_recv,
):
    n_dev = n_row * n_col
    my_row = lax.axis_index("row")
    my_col = lax.axis_index("col")
    me = my_row * n_col + my_col
    rows, width = v_hi.shape
    slots = disp_out.shape[1]
    flat = n_dev * slots
    blocks, terms, block = k_in.shape[0], k_in.shape[1], k_in.shape[2]
    pair = 2 * block
    pairs = rows // pair
    per_block = order_in.shape[0]

    def device(index):
        return (index // n_col, lax.rem(index, n_col))

    barrier = pltpu.get_barrier_semaphore()

    def greet(k, carry):
        pl.semaphore_signal(
            barrier, inc=1, device_id=device(lax.rem(me + k, n_dev)), device_id_type=MESH
        )
        return carry

    lax.fori_loop(1, n_dev, greet, 0)

    load_start = pltpu.make_async_copy(start_ref, vb.at[0], load_sem.at[0])
    load_k = pltpu.make_async_copy(k_ref, k_in, load_sem.at[1])
    load_mass = pltpu.make_async_copy(mass_hbm, mass_ref, load_sem.at[2])
    load_small = [
        pltpu.make_async_copy(source, target, load_sem.at[3 + i])
        for i, (source, target) in enumerate(
            ((panel_hbm, panel_ref), (low_hbm, low_ref), (high_hbm, high_ref), (cols_hbm, cols_ref))
        )
    ]
    for load in load_small:
        load.start()
    load_start.start()
    load_mass.start()
    load_k.start()
    for load in load_small:
        load.wait()

    def build_tables():
        def repeat(j, carry):
            named = lax.rem(j, n_col) * n_row + j // n_col
            spot = pl.ds(pl.multiple_of(j * slots, slots), slots)
            rep[spot, :] = jnp.broadcast_to(panel_ref[pl.ds(named, 1), :], (slots, per_block))
            return carry

        lax.fori_loop(0, n_dev, repeat, 0)
        cube = (n_dev, slots, per_block)
        slot_of = lax.broadcasted_iota(jnp.int32, cube, 1).reshape(flat, per_block)
        owner_of = lax.broadcasted_iota(jnp.int32, cube, 0).reshape(flat, per_block)
        lane = lax.broadcasted_iota(jnp.int32, (flat, per_block), 1)

        def hits(values, base):
            owned = (values >= base) & (values < base + rows)
            spot = jnp.where(owned, lane, per_block).astype(jnp.float32)
            first = jnp.min(spot, axis=1, keepdims=True).astype(jnp.int32)
            return owned & (lane - first == slot_of)

        values = rep[...]
        hit = hits(values, me * rows)
        local = jnp.where(hit, values - me * rows + 1, 0).astype(jnp.float32)
        local = jnp.sum(local, axis=1, keepdims=True) - 1.0
        across = jnp.broadcast_to(local, (flat, per_block)).T[0:1, :].astype(jnp.int32)
        down = local.astype(jnp.int32)
        one = jnp.ones((), jnp.float32)
        zero = jnp.zeros((), jnp.float32)
        wide = lax.broadcasted_iota(jnp.int32, (flat, rows), 1)
        pick[...] = jnp.where(wide == down, one, zero).astype(jnp.bfloat16)
        tall = lax.broadcasted_iota(jnp.int32, (rows, flat), 0)
        place[...] = jnp.where(tall == across, one, zero).astype(jnp.bfloat16)
        mine = jnp.broadcast_to(
            panel_ref[pl.ds(my_col * n_row + my_row, 1), :], (flat, per_block)
        )
        order = jnp.where(hits(mine, owner_of * rows), one, zero)
        order_out[...] = order.astype(jnp.bfloat16)
        order_in[...] = order.T.astype(jnp.bfloat16)

    lower = low_ref[...].astype(jnp.float32) * 0.25
    upper = high_ref[...].astype(jnp.float32) * 0.25
    centre[...] = 0.5 * (upper + lower)
    inverse[...] = 1.0 / (0.5 * (upper - lower))
    norm[...] = jnp.ones_like(norm)
    build_tables()
    pl.semaphore_wait(barrier, n_dev - 1)

    def remote(source, target, send, recv, to):
        return pltpu.make_async_remote_copy(
            src_ref=source, dst_ref=target, send_sem=send, recv_sem=recv,
            device_id=to, device_id_type=MESH,
        )

    def far(k):
        below = n_col - 1 - k
        below = jnp.where(below <= my_col, below - 1, below)
        above = jnp.where(k >= my_col, k + 1, k)
        return jnp.where(2 * my_col < n_col, below, above)

    def everyone(act):
        def line(k, first):
            row = lax.rem(my_row + k, n_row)
            for j in range(first, n_col):
                col = lax.rem(my_col + j, n_col)
                act(row * n_col + col, (row, col))

        def step(k, carry):
            line(k, 0)
            return carry

        lax.fori_loop(1, n_row, step, 0)
        line(0, 1)

    partner = my_row + 1 - 2 * lax.rem(my_row, 2)

    def wait_everyone(out, into, send, recv):
        others = pl.ds(0, n_dev - 1)
        remote(out.at[others], into.at[others], send, recv, (partner, my_col)).wait()

    def first_copy(to, where):
        return remote(first_out.at[to], first_in.at[me], first_send.at[0], first_recv.at[0], where)

    def coded_copies(out, out_s, into, into_s, send, recv, slot, to, where):
        return (
            remote(out.at[to], into.at[slot, me], send.at[0], recv.at[slot, 0], where),
            remote(out_s.at[to], into_s.at[slot, me], send.at[1], recv.at[slot, 1], where),
        )

    disp_copies = functools.partial(
        coded_copies, disp_out, disp_s, disp_in, disp_si, disp_send, disp_recv
    )
    ret_copies = functools.partial(
        coded_copies, ret_out, ret_s, ret_in, ret_si, ret_send, ret_recv
    )

    def exchange_start(copies, slot):
        def act(to, where):
            for copy in copies(slot, to, where):
                copy.start()

        everyone(act)

    def disp_wait(slot):
        wait_everyone(disp_out, disp_in.at[slot], disp_send.at[0], disp_recv.at[slot, 0])
        wait_everyone(disp_s, disp_si.at[slot], disp_send.at[1], disp_recv.at[slot, 1])

    def ret_wait(slot):
        wait_everyone(ret_out, ret_in.at[slot], ret_send.at[0], ret_recv.at[slot, 0])
        wait_everyone(ret_s, ret_si.at[slot], ret_send.at[1], ret_recv.at[slot, 1])

    def scatter_coded(value, out, out_s, into, into_s, copies, slot):
        coded, scale = encode(value.reshape(n_dev, slots, width), 1)
        out[...] = coded
        out_s[...] = scale
        exchange_start(copies, slot)
        into[slot, me] = out[me]
        into_s[slot, me] = out_s[me]

    def collect(into, into_s, slot):
        return split(decode(into[slot], into_s[slot]).reshape(flat, width))

    chips = n_row // 2

    def wet_copy(k):
        to = (lax.rem(my_row + 2 * k, n_row), my_col)
        return remote(wet.at[my_row], wet.at[my_row], wet_send.at[k], wet_recv.at[k], to)

    def wet_forward(k):
        held = wet.at[lax.rem(my_row + n_row - 2 * k, n_row)]
        return remote(
            held, held, wet_send.at[chips + k], wet_recv.at[chips + k], (partner, my_col)
        )

    def gather_start():
        for k in range(1, chips):
            wet_copy(k).start()
        wet_forward(0).start()

    def gather_wait():
        for k in range(1, chips):
            wet_copy(k).wait_recv()
            wet_forward(k).start()
        for k in range(1, chips):
            wet_copy(k).wait_send()
        for k in range(chips):
            wet_forward(k).wait()

    def rs_copies(to):
        where = (my_row, to)
        return (
            remote(rs_out.at[to], rs_in.at[my_col], rs_send.at[0], rs_recv.at[0], where),
            remote(rs_s.at[to], rs_si.at[my_col], rs_send.at[1], rs_recv.at[1], where),
        )

    def product_start():
        gathered = wet[...].reshape(n_row * per_block, width)

        def product(index):
            chunk = pl.ds(pl.multiple_of(index * per_block, per_block), per_block)
            return dot(mass[chunk, :], gathered)

        for k in range(n_col - 1):
            other = far(k)
            coded, scale = encode(product(other), 0)
            rs_out[other] = coded
            rs_s[other] = scale
            for copy in rs_copies(other):
                copy.start()
        pressure[...] = product(my_col)

    def product_wait():
        others = pl.ds(0, n_col - 1)
        where = (partner, my_col)
        remote(rs_out.at[others], rs_in.at[others], rs_send.at[0], rs_recv.at[0], where).wait()
        remote(rs_s.at[others], rs_si.at[others], rs_send.at[1], rs_recv.at[1], where).wait()
        total = pressure[...]
        for k in range(1, n_col):
            other = lax.rem(my_col + k, n_col)
            total = total + decode(rs_in[other], rs_si[other])
        pressure[...] = total

    def halo_copies(side):
        where = device(lax.rem(me + 1 + side * (n_dev - 2), n_dev))
        return (
            remote(
                halo_out.at[side], halo_in.at[side], halo_send.at[0, side], halo_recv.at[0, side],
                where,
            ),
            remote(
                halo_s.at[side], halo_si.at[side], halo_send.at[1, side], halo_recv.at[1, side],
                where,
            ),
        )

    def halo_start(slot):
        lead = jnp.where(my_col == 0, 1, 0)
        for turn in range(2):
            side = lead if turn == 0 else 1 - lead
            spot = pl.multiple_of((1 - side) * (rows - pair), pair)
            coded, scale = encode(vb[slot, pl.ds(spot, pair), :], 0)
            halo_out[side] = coded
            halo_s[side] = scale
            for copy in halo_copies(side):
                copy.start()

    def banded(q, first, values_hi, values_lo):
        count = values_hi.shape[0]
        window_hi = k_hi[q, :, first : first + count]
        window_lo = k_lo[q, :, first : first + count]
        return (
            dot(window_hi, values_hi) + dot(window_lo, values_hi) + dot(window_hi, values_lo)
        )

    def build_band():
        for q in range(pairs):
            for half in range(2):
                i = 2 * q + half
                base = me * blocks - 2 + 2 * q
                for o in range(6):
                    total = jnp.zeros((block, block), jnp.float32)
                    for k in range(terms):
                        flag = (cols_ref[k, i] - base == o).astype(jnp.float32)
                        total = total + k_in[i, k] * flag
                    high, low = split(total)
                    k_hi[q, half * block : (half + 1) * block, o * block : (o + 1) * block] = high
                    k_lo[q, half * block : (half + 1) * block, o * block : (o + 1) * block] = low

    def inner_stiffness():
        for q in range(pairs):
            first = max(q - 1, 0) * pair
            last = min(q + 2, pairs) * pair
            stiff[q * pair : (q + 1) * pair, :] = banded(
                q, pair if q == 0 else 0, v_hi[first:last, :], v_lo[first:last, :]
            )

    def outer_stiffness():
        for side in range(2):
            for copy in halo_copies(side):
                copy.wait()
        high, low = split(decode(halo_in[0], halo_si[0]))
        stiff[0:pair, :] += banded(0, 0, high, low)
        high, low = split(decode(halo_in[1], halo_si[1]))
        stiff[rows - pair : rows, :] += banded(pairs - 1, 2 * pair, high, low)

    def alpha(step):
        start = lax.rem(step, DEGREE) == 0
        factor = jnp.where(start, 1.0, 2.0).astype(jnp.float32)
        scaled = start & (step > 0)
        return inverse[...] * factor * jnp.where(scaled, norm[...], 1.0)

    def beta(step):
        place_in = lax.rem(step, DEGREE)
        factor = jnp.where(place_in == 0, 0.0, 1.0).astype(jnp.float32)
        scaled = (place_in == 1) & (step > 1)
        return factor * jnp.where(scaled, norm[...], 1.0)

    def known_part(step, slot):
        mine = alpha(step) * (stiff[...] - centre[...] * vb[slot])
        mine = mine - beta(step) * vb[1 - slot]
        stiff[...] = mine

    def send_known(step):
        high, low = split(stiff[...])
        chosen = dot(pick[...], high) + dot(pick[...], low)
        scatter_coded(
            chosen, disp_out, disp_s, disp_in, disp_si, disp_copies, lax.rem(step, 2)
        )

    def send_pressure(slot):
        high, low = split(pressure[...])
        ordered = dot(order_out[...], high) + dot(order_out[...], low)
        scatter_coded(ordered, ret_out, ret_s, ret_in, ret_si, ret_copies, slot)

    def next_values(step, slot):
        parity = lax.rem(step, 2)
        ret_wait(parity)
        high, low = collect(ret_in, ret_si, parity)
        loads = dot(place[...], high) + dot(place[...], low)
        vb[1 - slot] = stiff[...] + alpha(step) * loads

    def square_start(outer, panels):
        shells = stiff[...] * dry[...]
        sq_out[...] = jnp.sum(shells * shells, axis=0, keepdims=True) + jnp.sum(
            panels * panels, axis=0, keepdims=True
        )

        def act(to, where):
            remote(sq_out, sq_in.at[outer, me], sq_send.at[outer], sq_recv.at[outer], where).start()

        everyone(act)
        sq_in[outer, me] = sq_out[...]

    def square_wait(outer):
        arrived = sq_in.at[outer]
        wait_everyone(arrived, arrived, sq_send.at[outer], sq_recv.at[outer])
        squares = jnp.sum(sq_in[outer], axis=0)
        return 1.0 / jnp.sqrt(squares / (rows * n_dev) + 1e-06)

    def panel_values(step):
        slot = lax.rem(step, 2)
        disp_wait(slot)
        high, low = collect(disp_in, disp_si, slot)
        known = dot(order_in[...], high) + dot(order_in[...], low)
        return known + alpha(step) * pressure[...]

    def split_values(slot):
        high, low = split(vb[slot])
        v_hi[...] = high
        v_lo[...] = low

    def mass_place(i):
        index = n_col * my_row + i
        to = lax.rem(index, n_row)
        source = mass_ref.at[pl.ds(i * per_block, per_block), :]
        spot = pl.multiple_of((index // n_row) * per_block, per_block)
        return to, source, mass.at[pl.ds(spot, per_block), :], index // n_row

    def mass_start(wave):
        for i in range(wave, n_col, 2):
            to, source, target, spot = mass_place(i)

            @pl.when(to != my_row)
            def _():
                remote(source, target, mass_send.at[i], mass_recv.at[spot], (to, my_col)).start()

            @pl.when(to == my_row)
            def _():
                pltpu.make_async_copy(source, target, mass_send.at[i]).start()

    def mass_wait():
        for i in range(n_col):
            to, source, target, spot = mass_place(i)

            @pl.when(to != my_row)
            def _():
                remote(
                    source, target, mass_send.at[i], mass_recv.at[spot], (to, my_col)
                ).wait_send()

            @pl.when(to == my_row)
            def _():
                pltpu.make_async_copy(source, target, mass_send.at[i]).wait()

        for q in range(n_col):
            index = q * n_row + my_row
            target = mass.at[pl.ds(q * per_block, per_block), :]
            source = mass_ref.at[pl.ds(0, per_block), :]

            @pl.when(index // n_col != my_row)
            def _():
                remote(
                    source, target, mass_send.at[q], mass_recv.at[q], (index // n_col, my_col)
                ).wait_recv()

    load_start.wait()
    split_values(0)
    first_out[...] = dot(pick[...], v_hi[...]).reshape(n_dev, slots, width).astype(jnp.bfloat16)
    everyone(lambda to, where: first_copy(to, where).start())
    first_in[me] = first_out[me]
    halo_start(0)
    load_mass.wait()
    mass_start(0)
    load_k.wait()
    build_band()
    inner_stiffness()
    ones = jnp.ones((flat, width), jnp.bfloat16)
    dry[...] = 1.0 - dot(place[...], ones)
    wait_everyone(first_out, first_in, first_send.at[0], first_recv.at[0])
    arrived = first_in[...].astype(jnp.float32).reshape(flat, width).astype(jnp.bfloat16)
    wet[my_row] = dot(order_in[...], arrived).astype(jnp.bfloat16)
    gather_start()
    mass_start(1)
    outer_stiffness()
    gather_wait()
    mass_wait()
    product_start()
    known_part(0, 0)
    send_known(0)
    product_wait()

    def step_of(step, carry):
        slot = lax.rem(step, 2)
        ends = lax.rem(step, DEGREE) == DEGREE - 1
        outer = step // DEGREE
        send_pressure(slot)
        panels = panel_values(step)
        wet[my_row] = panels.astype(jnp.bfloat16)
        gather_start()

        @pl.when(ends)
        def _():
            square_start(outer, panels)

        next_values(step, slot)
        halo_start(1 - slot)
        split_values(1 - slot)
        gather_wait()
        product_start()
        inner_stiffness()
        outer_stiffness()

        @pl.when(ends)
        def _():
            norm[...] = square_wait(outer)

        known_part(step + 1, 1 - slot)
        send_known(step + 1)
        product_wait()
        return carry

    lax.fori_loop(0, STEPS - 1, step_of, 0)
    last = STEPS - 1
    slot = last % 2
    send_pressure(slot)
    square_start(OUTER - 1, panel_values(last))
    next_values(last, slot)
    store = pltpu.make_async_copy(vb.at[1 - slot], result_ref, load_sem.at[0])
    store.start()
    scale_ref[...] = square_wait(OUTER - 1)
    store.wait()


def body(mode_block, k_blocks, block_cols, panel_node, added_mass, low_edge, high_edge):
    n_row = lax.axis_size("row")
    n_col = lax.axis_size("col")
    devices = n_row * n_col
    rows_dev, width = mode_block.shape
    block_size = k_blocks.shape[2]
    per_block = panel_node.shape[0] // devices
    most = 2 * ((per_block + devices - 1) // devices)
    slots = (most + SUBLANES - 1) // SUBLANES * SUBLANES
    flat = devices * slots
    pair = 2 * block_size
    pairs = rows_dev // pair
    f32, bf16, i16 = jnp.float32, jnp.bfloat16, jnp.int16
    vmem = pl.BlockSpec(memory_space=pltpu.VMEM)
    anywhere = pl.BlockSpec(memory_space=pl.ANY)
    dma = pltpu.SemaphoreType.DMA
    coded = pltpu.VMEM((devices, slots, width), i16)
    coded_in = pltpu.VMEM((2, devices, slots, width), i16)
    scale = pltpu.VMEM((devices, 1, width), f32)
    scale_in = pltpu.VMEM((2, devices, 1, width), f32)
    row = pltpu.VMEM((1, width), f32)
    values, factor = pl.pallas_call(
        functools.partial(kernel, n_row, n_col),
        out_shape=(
            jax.ShapeDtypeStruct(mode_block.shape, f32),
            jax.ShapeDtypeStruct((1, width), f32),
        ),
        in_specs=[anywhere] * 7,
        out_specs=(anywhere, vmem),
        scratch_shapes=[
            pltpu.SMEM(block_cols.shape[::-1], jnp.int32),
            pltpu.VMEM((devices, per_block), jnp.int32),
            pltpu.VMEM((1, width), jnp.int32),
            pltpu.VMEM((1, width), jnp.int32),
            pltpu.VMEM(added_mass.shape, bf16),
            pltpu.VMEM((2, rows_dev, width), f32),
            pltpu.VMEM((rows_dev, width), bf16),
            pltpu.VMEM((rows_dev, width), bf16),
            pltpu.VMEM((rows_dev, width), f32),
            pltpu.VMEM(k_blocks.shape, f32),
            pltpu.VMEM((pairs, pair, 3 * pair), bf16),
            pltpu.VMEM((pairs, pair, 3 * pair), bf16),
            pltpu.VMEM(added_mass.shape, bf16),
            pltpu.VMEM((flat, per_block), jnp.int32),
            pltpu.VMEM((flat, rows_dev), bf16),
            pltpu.VMEM((rows_dev, flat), bf16),
            pltpu.VMEM((per_block, flat), bf16),
            pltpu.VMEM((flat, per_block), bf16),
            pltpu.VMEM((devices, slots, width), bf16),
            pltpu.VMEM((devices, slots, width), bf16),
            coded, coded_in, scale, scale_in,
            pltpu.VMEM((n_row, per_block, width), bf16),
            pltpu.VMEM((n_col, per_block, width), i16),
            pltpu.VMEM((n_col, per_block, width), i16),
            pltpu.VMEM((n_col, 1, width), f32),
            pltpu.VMEM((n_col, 1, width), f32),
            pltpu.VMEM((per_block, width), f32),
            coded, coded_in, scale, scale_in,
            pltpu.VMEM((2, pair, width), i16),
            pltpu.VMEM((2, pair, width), i16),
            pltpu.VMEM((2, 1, width), f32),
            pltpu.VMEM((2, 1, width), f32),
            row, row, row, row,
            pltpu.VMEM((OUTER, devices, 1, width), f32),
            pltpu.VMEM((rows_dev, width), f32),
            dma((7,)),
            dma((n_col,)),
            dma((n_col,)),
            dma((1,)),
            dma((1,)),
            dma((2,)),
            dma((2, 2)),
            dma((n_row,)),
            dma((n_row,)),
            dma((2,)),
            dma((2,)),
            dma((2,)),
            dma((2, 2)),
            dma((2, 2)),
            dma((2, 2)),
            dma((OUTER,)),
            dma((OUTER,)),
        ],
        compiler_params=pltpu.CompilerParams(
            collective_id=0, has_side_effects=True, vmem_limit_bytes=60 * 1024 * 1024
        ),
    )(
        block_cols.T,
        panel_node.reshape(devices, per_block),
        low_edge.reshape(1, width),
        high_edge.reshape(1, width),
        mode_block,
        k_blocks,
        added_mass,
    )
    return values * factor


def solution(mesh):
    placed = (
        P(("row", "col"), None),
        P(("row", "col"), None, None, None),
        P(("row", "col"), None),
        P(),
        P("row", "col"),
        P(),
        P(),
    )
    return jax.shard_map(
        body, mesh=mesh, in_specs=placed, out_specs=P(("row", "col"), None), check_vma=False
    )
```

```python
import functools

import jax
import jax.numpy as jnp
from jax import lax
from jax.experimental import pallas as pl
from jax.experimental.pallas import tpu as pltpu
from jax.sharding import PartitionSpec as P

DEGREE = 3
OUTER = 2
STEPS = DEGREE * OUTER
SUBLANES = 8
LIMIT = 32767.0
MESH = pl.DeviceIdType.MESH


def dot(left, right):
    return jnp.dot(left, right, preferred_element_type=jnp.float32)


def split(value):
    high = value.astype(jnp.bfloat16)
    low = (value - high.astype(jnp.float32)).astype(jnp.bfloat16)
    return high, low


def encode(value, axis):
    largest = jnp.maximum(jnp.max(jnp.abs(value), axis=axis, keepdims=True), 1e-30)
    coded = jnp.round(value * (LIMIT / largest))
    return coded.astype(jnp.int32).astype(jnp.int16), largest * (1.0 / LIMIT)


def decode(coded, scale):
    return coded.astype(jnp.int32).astype(jnp.float32) * scale


def kernel(
    n_row, n_col,
    cols_hbm, panel_hbm, low_hbm, high_hbm, start_ref, k_ref, mass_hbm,
    result_ref, scale_ref,
    cols_ref, panel_ref, low_ref, high_ref, mass_ref, vb, v_hi, v_lo, stiff, k_in, k_hi, k_lo, mass, rep, pick, place, order_in, order_out,
    first_out, first_in, disp_out, disp_in, disp_s, disp_si, wet,
    rs_out, rs_in, rs_s, rs_si, pressure,
    ret_out, ret_in, ret_s, ret_si, halo_out, halo_in, halo_s, halo_si,
    centre, inverse, norm, sq_out, sq_in, dry, chosen_part,
    load_sem, mass_send, mass_recv, first_send, first_recv, disp_send, disp_recv, wet_send, wet_recv,
    rs_send, rs_recv, ret_send, ret_recv, halo_send, halo_recv, sq_send, sq_recv,
):
    n_dev = n_row * n_col
    my_row = lax.axis_index("row")
    my_col = lax.axis_index("col")
    me = my_row * n_col + my_col
    rows, width = v_hi.shape
    slots = disp_out.shape[1]
    flat = n_dev * slots
    blocks, terms, block = k_in.shape[0], k_in.shape[1], k_in.shape[2]
    pair = 2 * block
    pairs = rows // pair
    per_block = order_in.shape[0]

    def device(index):
        return (index // n_col, lax.rem(index, n_col))

    barrier = pltpu.get_barrier_semaphore()

    def greet(k, carry):
        pl.semaphore_signal(
            barrier, inc=1, device_id=device(lax.rem(me + k, n_dev)), device_id_type=MESH
        )
        return carry

    lax.fori_loop(1, n_dev, greet, 0)

    load_start = pltpu.make_async_copy(start_ref, vb.at[0], load_sem.at[0])
    load_k = pltpu.make_async_copy(k_ref, k_in, load_sem.at[1])
    load_mass = pltpu.make_async_copy(mass_hbm, mass_ref, load_sem.at[2])
    load_small = [
        pltpu.make_async_copy(source, target, load_sem.at[3 + i])
        for i, (source, target) in enumerate(
            ((panel_hbm, panel_ref), (low_hbm, low_ref), (high_hbm, high_ref), (cols_hbm, cols_ref))
        )
    ]
    for load in load_small:
        load.start()
    load_start.start()
    load_mass.start()
    load_k.start()
    for load in load_small:
        load.wait()

    def build_tables():
        def repeat(j, carry):
            named = lax.rem(j, n_col) * n_row + j // n_col
            spot = pl.ds(pl.multiple_of(j * slots, slots), slots)
            rep[spot, :] = jnp.broadcast_to(panel_ref[pl.ds(named, 1), :], (slots, per_block))
            return carry

        lax.fori_loop(0, n_dev, repeat, 0)
        cube = (n_dev, slots, per_block)
        slot_of = lax.broadcasted_iota(jnp.int32, cube, 1).reshape(flat, per_block)
        owner_of = lax.broadcasted_iota(jnp.int32, cube, 0).reshape(flat, per_block)
        lane = lax.broadcasted_iota(jnp.int32, (flat, per_block), 1)

        def hits(values, base):
            owned = (values >= base) & (values < base + rows)
            spot = jnp.where(owned, lane, per_block).astype(jnp.float32)
            first = jnp.min(spot, axis=1, keepdims=True).astype(jnp.int32)
            return owned & (lane - first == slot_of)

        values = rep[...]
        hit = hits(values, me * rows)
        local = jnp.where(hit, values - me * rows + 1, 0).astype(jnp.float32)
        local = jnp.sum(local, axis=1, keepdims=True) - 1.0
        across = jnp.broadcast_to(local, (flat, per_block)).T[0:1, :].astype(jnp.int32)
        down = local.astype(jnp.int32)
        one = jnp.ones((), jnp.float32)
        zero = jnp.zeros((), jnp.float32)
        wide = lax.broadcasted_iota(jnp.int32, (flat, rows), 1)
        pick[...] = jnp.where(wide == down, one, zero).astype(jnp.bfloat16)
        tall = lax.broadcasted_iota(jnp.int32, (rows, flat), 0)
        place[...] = jnp.where(tall == across, one, zero).astype(jnp.bfloat16)
        mine = jnp.broadcast_to(
            panel_ref[pl.ds(my_col * n_row + my_row, 1), :], (flat, per_block)
        )
        order = jnp.where(hits(mine, owner_of * rows), one, zero)
        order_out[...] = order.astype(jnp.bfloat16)
        order_in[...] = order.T.astype(jnp.bfloat16)

    lower = low_ref[...].astype(jnp.float32) * 0.25
    upper = high_ref[...].astype(jnp.float32) * 0.25
    centre[...] = 0.5 * (upper + lower)
    inverse[...] = 1.0 / (0.5 * (upper - lower))
    norm[...] = jnp.ones_like(norm)
    build_tables()
    pl.semaphore_wait(barrier, n_dev - 1)

    def remote(source, target, send, recv, to):
        return pltpu.make_async_remote_copy(
            src_ref=source, dst_ref=target, send_sem=send, recv_sem=recv,
            device_id=to, device_id_type=MESH,
        )

    def far(k):
        below = n_col - 1 - k
        below = jnp.where(below <= my_col, below - 1, below)
        above = jnp.where(k >= my_col, k + 1, k)
        return jnp.where(2 * my_col < n_col, below, above)

    def everyone(act):
        def line(k, first):
            row = lax.rem(my_row + k, n_row)
            for j in range(first, n_col):
                col = lax.rem(my_col + j, n_col)
                act(row * n_col + col, (row, col))

        def step(k, carry):
            line(k, 0)
            return carry

        lax.fori_loop(1, n_row, step, 0)
        line(0, 1)

    partner = my_row + 1 - 2 * lax.rem(my_row, 2)

    def wait_everyone(out, into, send, recv):
        others = pl.ds(0, n_dev - 1)
        remote(out.at[others], into.at[others], send, recv, (partner, my_col)).wait()

    def first_copy(to, where):
        return remote(first_out.at[to], first_in.at[me], first_send.at[0], first_recv.at[0], where)

    def coded_copies(out, out_s, into, into_s, send, recv, slot, to, where):
        return (
            remote(out.at[to], into.at[slot, me], send.at[0], recv.at[slot, 0], where),
            remote(out_s.at[to], into_s.at[slot, me], send.at[1], recv.at[slot, 1], where),
        )

    disp_copies = functools.partial(
        coded_copies, disp_out, disp_s, disp_in, disp_si, disp_send, disp_recv
    )
    ret_copies = functools.partial(
        coded_copies, ret_out, ret_s, ret_in, ret_si, ret_send, ret_recv
    )

    def exchange_start(copies, slot):
        def act(to, where):
            for copy in copies(slot, to, where):
                copy.start()

        everyone(act)

    def disp_wait(slot):
        wait_everyone(disp_out, disp_in.at[slot], disp_send.at[0], disp_recv.at[slot, 0])
        wait_everyone(disp_s, disp_si.at[slot], disp_send.at[1], disp_recv.at[slot, 1])

    def ret_wait(slot):
        wait_everyone(ret_out, ret_in.at[slot], ret_send.at[0], ret_recv.at[slot, 0])
        wait_everyone(ret_s, ret_si.at[slot], ret_send.at[1], ret_recv.at[slot, 1])

    def scatter_coded(value, out, out_s, into, into_s, copies, slot):
        coded, scale = encode(value.reshape(n_dev, slots, width), 1)
        out[...] = coded
        out_s[...] = scale
        exchange_start(copies, slot)
        into[slot, me] = out[me]
        into_s[slot, me] = out_s[me]

    def collect(into, into_s, slot):
        return split(decode(into[slot], into_s[slot]).reshape(flat, width))

    chips = n_row // 2

    def wet_copy(k):
        to = (lax.rem(my_row + 2 * k, n_row), my_col)
        return remote(wet.at[my_row], wet.at[my_row], wet_send.at[k], wet_recv.at[k], to)

    def wet_forward(k):
        held = wet.at[lax.rem(my_row + n_row - 2 * k, n_row)]
        return remote(
            held, held, wet_send.at[chips + k], wet_recv.at[chips + k], (partner, my_col)
        )

    def gather_start():
        for k in range(1, chips):
            wet_copy(k).start()
        wet_forward(0).start()

    def gather_wait():
        for k in range(1, chips):
            wet_copy(k).wait_recv()
            wet_forward(k).start()
        for k in range(1, chips):
            wet_copy(k).wait_send()
        for k in range(chips):
            wet_forward(k).wait()

    def rs_copies(to):
        where = (my_row, to)
        return (
            remote(rs_out.at[to], rs_in.at[my_col], rs_send.at[0], rs_recv.at[0], where),
            remote(rs_s.at[to], rs_si.at[my_col], rs_send.at[1], rs_recv.at[1], where),
        )

    def product_start():
        gathered = wet[...].reshape(n_row * per_block, width)

        def product(index):
            chunk = pl.ds(pl.multiple_of(index * per_block, per_block), per_block)
            return dot(mass[chunk, :], gathered)

        for k in range(n_col - 1):
            other = far(k)
            coded, scale = encode(product(other), 0)
            rs_out[other] = coded
            rs_s[other] = scale
            for copy in rs_copies(other):
                copy.start()
        pressure[...] = product(my_col)

    def product_wait():
        others = pl.ds(0, n_col - 1)
        where = (partner, my_col)
        remote(rs_out.at[others], rs_in.at[others], rs_send.at[0], rs_recv.at[0], where).wait()
        remote(rs_s.at[others], rs_si.at[others], rs_send.at[1], rs_recv.at[1], where).wait()
        total = pressure[...]
        for k in range(1, n_col):
            other = lax.rem(my_col + k, n_col)
            total = total + decode(rs_in[other], rs_si[other])
        pressure[...] = total

    def halo_copies(side):
        where = device(lax.rem(me + 1 + side * (n_dev - 2), n_dev))
        return (
            remote(
                halo_out.at[side], halo_in.at[side], halo_send.at[0, side], halo_recv.at[0, side],
                where,
            ),
            remote(
                halo_s.at[side], halo_si.at[side], halo_send.at[1, side], halo_recv.at[1, side],
                where,
            ),
        )

    def halo_start(slot):
        lead = jnp.where(my_col == 0, 1, 0)
        for turn in range(2):
            side = lead if turn == 0 else 1 - lead
            spot = pl.multiple_of((1 - side) * (rows - pair), pair)
            coded, scale = encode(vb[slot, pl.ds(spot, pair), :], 0)
            halo_out[side] = coded
            halo_s[side] = scale
            for copy in halo_copies(side):
                copy.start()

    def banded(q, first, values_hi, values_lo):
        count = values_hi.shape[0]
        window_hi = k_hi[q, :, first : first + count]
        window_lo = k_lo[q, :, first : first + count]
        return (
            dot(window_hi, values_hi) + dot(window_lo, values_hi) + dot(window_hi, values_lo)
        )

    def build_band():
        for q in range(pairs):
            for half in range(2):
                i = 2 * q + half
                base = me * blocks - 2 + 2 * q
                for o in range(6):
                    total = jnp.zeros((block, block), jnp.float32)
                    for k in range(terms):
                        flag = (cols_ref[k, i] - base == o).astype(jnp.float32)
                        total = total + k_in[i, k] * flag
                    high, low = split(total)
                    k_hi[q, half * block : (half + 1) * block, o * block : (o + 1) * block] = high
                    k_lo[q, half * block : (half + 1) * block, o * block : (o + 1) * block] = low

    def inner_stiffness():
        for q in range(pairs):
            first = max(q - 1, 0) * pair
            last = min(q + 2, pairs) * pair
            stiff[q * pair : (q + 1) * pair, :] = banded(
                q, pair if q == 0 else 0, v_hi[first:last, :], v_lo[first:last, :]
            )

    def outer_stiffness():
        for side in range(2):
            for copy in halo_copies(side):
                copy.wait()
        high, low = split(decode(halo_in[0], halo_si[0]))
        stiff[0:pair, :] += banded(0, 0, high, low)
        high, low = split(decode(halo_in[1], halo_si[1]))
        stiff[rows - pair : rows, :] += banded(pairs - 1, 2 * pair, high, low)

    def alpha(step):
        start = lax.rem(step, DEGREE) == 0
        factor = jnp.where(start, 1.0, 2.0).astype(jnp.float32)
        scaled = start & (step > 0)
        return inverse[...] * factor * jnp.where(scaled, norm[...], 1.0)

    def beta(step):
        place_in = lax.rem(step, DEGREE)
        factor = jnp.where(place_in == 0, 0.0, 1.0).astype(jnp.float32)
        scaled = (place_in == 1) & (step > 1)
        return factor * jnp.where(scaled, norm[...], 1.0)

    def known_part(step, slot, first, last):
        mine = alpha(step) * (stiff[first:last, :] - centre[...] * vb[slot, first:last, :])
        mine = mine - beta(step) * vb[1 - slot, first:last, :]
        stiff[first:last, :] = mine
        high, low = split(mine)
        return dot(pick[:, first:last], high) + dot(pick[:, first:last], low)

    def known_inner(step, slot):
        chosen_part[...] = known_part(step, slot, pair, rows - pair)

    def send_known(step, slot):
        chosen = chosen_part[...] + known_part(step, slot, 0, pair)
        chosen = chosen + known_part(step, slot, rows - pair, rows)
        scatter_coded(
            chosen, disp_out, disp_s, disp_in, disp_si, disp_copies, lax.rem(step, 2)
        )

    def send_pressure(slot):
        high, low = split(pressure[...])
        ordered = dot(order_out[...], high) + dot(order_out[...], low)
        scatter_coded(ordered, ret_out, ret_s, ret_in, ret_si, ret_copies, slot)

    def next_values(step, slot, edges):
        parity = lax.rem(step, 2)
        ret_wait(parity)
        high, low = collect(ret_in, ret_si, parity)

        def update(first, last):
            loads = dot(place[first:last, :], high) + dot(place[first:last, :], low)
            vb[1 - slot, first:last, :] = stiff[first:last, :] + alpha(step) * loads

        update(0, pair)
        update(rows - pair, rows)
        if edges:
            halo_start(1 - slot)
        update(pair, rows - pair)

    def square_start(outer, panels):
        shells = stiff[...] * dry[...]
        sq_out[...] = jnp.sum(shells * shells, axis=0, keepdims=True) + jnp.sum(
            panels * panels, axis=0, keepdims=True
        )

        def act(to, where):
            remote(sq_out, sq_in.at[outer, me], sq_send.at[outer], sq_recv.at[outer], where).start()

        everyone(act)
        sq_in[outer, me] = sq_out[...]

    def square_wait(outer):
        arrived = sq_in.at[outer]
        wait_everyone(arrived, arrived, sq_send.at[outer], sq_recv.at[outer])
        squares = jnp.sum(sq_in[outer], axis=0)
        return 1.0 / jnp.sqrt(squares / (rows * n_dev) + 1e-06)

    def panel_values(step):
        slot = lax.rem(step, 2)
        disp_wait(slot)
        high, low = collect(disp_in, disp_si, slot)
        known = dot(order_in[...], high) + dot(order_in[...], low)
        return known + alpha(step) * pressure[...]

    def split_values(slot):
        high, low = split(vb[slot])
        v_hi[...] = high
        v_lo[...] = low

    def mass_place(i):
        index = n_col * my_row + i
        to = lax.rem(index, n_row)
        source = mass_ref.at[pl.ds(i * per_block, per_block), :]
        spot = pl.multiple_of((index // n_row) * per_block, per_block)
        return to, source, mass.at[pl.ds(spot, per_block), :], index // n_row

    def mass_start(wave):
        for i in range(wave, n_col, 2):
            to, source, target, spot = mass_place(i)

            @pl.when(to != my_row)
            def _():
                remote(source, target, mass_send.at[i], mass_recv.at[spot], (to, my_col)).start()

            @pl.when(to == my_row)
            def _():
                pltpu.make_async_copy(source, target, mass_send.at[i]).start()

    def mass_wait():
        for i in range(n_col):
            to, source, target, spot = mass_place(i)

            @pl.when(to != my_row)
            def _():
                remote(
                    source, target, mass_send.at[i], mass_recv.at[spot], (to, my_col)
                ).wait_send()

            @pl.when(to == my_row)
            def _():
                pltpu.make_async_copy(source, target, mass_send.at[i]).wait()

        for q in range(n_col):
            index = q * n_row + my_row
            target = mass.at[pl.ds(q * per_block, per_block), :]
            source = mass_ref.at[pl.ds(0, per_block), :]

            @pl.when(index // n_col != my_row)
            def _():
                remote(
                    source, target, mass_send.at[q], mass_recv.at[q], (index // n_col, my_col)
                ).wait_recv()

    load_start.wait()
    split_values(0)
    first_out[...] = dot(pick[...], v_hi[...]).reshape(n_dev, slots, width).astype(jnp.bfloat16)
    everyone(lambda to, where: first_copy(to, where).start())
    first_in[me] = first_out[me]
    halo_start(0)
    load_mass.wait()
    mass_start(0)
    load_k.wait()
    build_band()
    inner_stiffness()
    ones = jnp.ones((flat, width), jnp.bfloat16)
    dry[...] = 1.0 - dot(place[...], ones)
    wait_everyone(first_out, first_in, first_send.at[0], first_recv.at[0])
    arrived = first_in[...].astype(jnp.float32).reshape(flat, width).astype(jnp.bfloat16)
    wet[my_row] = dot(order_in[...], arrived).astype(jnp.bfloat16)
    gather_start()
    mass_start(1)
    outer_stiffness()
    gather_wait()
    mass_wait()
    product_start()
    known_inner(0, 0)
    send_known(0, 0)
    product_wait()

    def step_of(step, carry):
        slot = lax.rem(step, 2)
        ends = lax.rem(step, DEGREE) == DEGREE - 1
        outer = step // DEGREE
        send_pressure(slot)
        panels = panel_values(step)
        wet[my_row] = panels.astype(jnp.bfloat16)
        gather_start()

        @pl.when(ends)
        def _():
            square_start(outer, panels)

        next_values(step, slot, True)
        split_values(1 - slot)
        gather_wait()
        product_start()
        inner_stiffness()

        @pl.when(ends)
        def _():
            norm[...] = square_wait(outer)

        known_inner(step + 1, 1 - slot)
        outer_stiffness()
        send_known(step + 1, 1 - slot)
        product_wait()
        return carry

    lax.fori_loop(0, STEPS - 1, step_of, 0)
    last = STEPS - 1
    slot = last % 2
    send_pressure(slot)
    square_start(OUTER - 1, panel_values(last))
    next_values(last, slot, False)
    store = pltpu.make_async_copy(vb.at[1 - slot], result_ref, load_sem.at[0])
    store.start()
    scale_ref[...] = square_wait(OUTER - 1)
    store.wait()


def body(mode_block, k_blocks, block_cols, panel_node, added_mass, low_edge, high_edge):
    n_row = lax.axis_size("row")
    n_col = lax.axis_size("col")
    devices = n_row * n_col
    rows_dev, width = mode_block.shape
    block_size = k_blocks.shape[2]
    per_block = panel_node.shape[0] // devices
    most = 2 * ((per_block + devices - 1) // devices)
    slots = (most + SUBLANES - 1) // SUBLANES * SUBLANES
    flat = devices * slots
    pair = 2 * block_size
    pairs = rows_dev // pair
    f32, bf16, i16 = jnp.float32, jnp.bfloat16, jnp.int16
    vmem = pl.BlockSpec(memory_space=pltpu.VMEM)
    anywhere = pl.BlockSpec(memory_space=pl.ANY)
    dma = pltpu.SemaphoreType.DMA
    coded = pltpu.VMEM((devices, slots, width), i16)
    coded_in = pltpu.VMEM((2, devices, slots, width), i16)
    scale = pltpu.VMEM((devices, 1, width), f32)
    scale_in = pltpu.VMEM((2, devices, 1, width), f32)
    row = pltpu.VMEM((1, width), f32)
    values, factor = pl.pallas_call(
        functools.partial(kernel, n_row, n_col),
        out_shape=(
            jax.ShapeDtypeStruct(mode_block.shape, f32),
            jax.ShapeDtypeStruct((1, width), f32),
        ),
        in_specs=[anywhere] * 7,
        out_specs=(anywhere, vmem),
        scratch_shapes=[
            pltpu.SMEM(block_cols.shape[::-1], jnp.int32),
            pltpu.VMEM((devices, per_block), jnp.int32),
            pltpu.VMEM((1, width), jnp.int32),
            pltpu.VMEM((1, width), jnp.int32),
            pltpu.VMEM(added_mass.shape, bf16),
            pltpu.VMEM((2, rows_dev, width), f32),
            pltpu.VMEM((rows_dev, width), bf16),
            pltpu.VMEM((rows_dev, width), bf16),
            pltpu.VMEM((rows_dev, width), f32),
            pltpu.VMEM(k_blocks.shape, f32),
            pltpu.VMEM((pairs, pair, 3 * pair), bf16),
            pltpu.VMEM((pairs, pair, 3 * pair), bf16),
            pltpu.VMEM(added_mass.shape, bf16),
            pltpu.VMEM((flat, per_block), jnp.int32),
            pltpu.VMEM((flat, rows_dev), bf16),
            pltpu.VMEM((rows_dev, flat), bf16),
            pltpu.VMEM((per_block, flat), bf16),
            pltpu.VMEM((flat, per_block), bf16),
            pltpu.VMEM((devices, slots, width), bf16),
            pltpu.VMEM((devices, slots, width), bf16),
            coded, coded_in, scale, scale_in,
            pltpu.VMEM((n_row, per_block, width), bf16),
            pltpu.VMEM((n_col, per_block, width), i16),
            pltpu.VMEM((n_col, per_block, width), i16),
            pltpu.VMEM((n_col, 1, width), f32),
            pltpu.VMEM((n_col, 1, width), f32),
            pltpu.VMEM((per_block, width), f32),
            coded, coded_in, scale, scale_in,
            pltpu.VMEM((2, pair, width), i16),
            pltpu.VMEM((2, pair, width), i16),
            pltpu.VMEM((2, 1, width), f32),
            pltpu.VMEM((2, 1, width), f32),
            row, row, row, row,
            pltpu.VMEM((OUTER, devices, 1, width), f32),
            pltpu.VMEM((rows_dev, width), f32),
            pltpu.VMEM((flat, width), f32),
            dma((7,)),
            dma((n_col,)),
            dma((n_col,)),
            dma((1,)),
            dma((1,)),
            dma((2,)),
            dma((2, 2)),
            dma((n_row,)),
            dma((n_row,)),
            dma((2,)),
            dma((2,)),
            dma((2,)),
            dma((2, 2)),
            dma((2, 2)),
            dma((2, 2)),
            dma((OUTER,)),
            dma((OUTER,)),
        ],
        compiler_params=pltpu.CompilerParams(
            collective_id=0, has_side_effects=True, vmem_limit_bytes=60 * 1024 * 1024
        ),
    )(
        block_cols.T,
        panel_node.reshape(devices, per_block),
        low_edge.reshape(1, width),
        high_edge.reshape(1, width),
        mode_block,
        k_blocks,
        added_mass,
    )
    return values * factor


def solution(mesh):
    placed = (
        P(("row", "col"), None),
        P(("row", "col"), None, None, None),
        P(("row", "col"), None),
        P(),
        P("row", "col"),
        P(),
        P(),
    )
    return jax.shard_map(
        body, mesh=mesh, in_specs=placed, out_specs=P(("row", "col"), None), check_vma=False
    )
```

```python
import functools

import jax
import jax.numpy as jnp
from jax import lax
from jax.experimental import pallas as pl
from jax.experimental.pallas import tpu as pltpu
from jax.sharding import PartitionSpec as P

DEGREE = 3
OUTER = 2
STEPS = DEGREE * OUTER
SUBLANES = 8
LIMIT = 32767.0
MARGIN = 1.004
MESH = pl.DeviceIdType.MESH


def dot(left, right):
    return jnp.dot(left, right, preferred_element_type=jnp.float32)


def split(value):
    high = value.astype(jnp.bfloat16)
    low = (value - high.astype(jnp.float32)).astype(jnp.bfloat16)
    return high, low


def encode(value, axis):
    largest = jnp.maximum(jnp.max(jnp.abs(value), axis=axis, keepdims=True), 1e-30)
    coded = jnp.round(value * (LIMIT / largest))
    return coded.astype(jnp.int32).astype(jnp.int16), largest * (1.0 / LIMIT)


def decode(coded, scale):
    return coded.astype(jnp.int32).astype(jnp.float32) * scale


def kernel(
    n_row, n_col,
    cols_hbm, panel_hbm, low_hbm, high_hbm, start_ref, k_ref, mass_hbm,
    result_ref, scale_ref,
    cols_ref, panel_ref, low_ref, high_ref, mass_ref, vb, v_hi, v_lo, stiff, k_in, k_hi, k_lo, mass, rep, pick, place, order_in, order_out,
    first_out, first_in, disp_out, disp_in, disp_s, disp_si, wet,
    rs_out, rs_in, rs_s, rs_si, pressure,
    ret_out, ret_in, ret_s, ret_si, halo_out, halo_in, halo_s, halo_si,
    centre, inverse, norm, sq_out, sq_in, dry, chosen_part,
    load_sem, mass_send, mass_recv, first_send, first_recv, disp_send, disp_recv, wet_send, wet_recv,
    rs_send, rs_recv, ret_send, ret_recv, halo_send, halo_recv, sq_send, sq_recv,
):
    n_dev = n_row * n_col
    my_row = lax.axis_index("row")
    my_col = lax.axis_index("col")
    me = my_row * n_col + my_col
    rows, width = v_hi.shape
    slots = disp_out.shape[1]
    flat = n_dev * slots
    blocks, terms, block = k_in.shape[0], k_in.shape[1], k_in.shape[2]
    pair = 2 * block
    pairs = rows // pair
    per_block = order_in.shape[0]

    def device(index):
        return (index // n_col, lax.rem(index, n_col))

    barrier = pltpu.get_barrier_semaphore()

    def greet(k, carry):
        pl.semaphore_signal(
            barrier, inc=1, device_id=device(lax.rem(me + k, n_dev)), device_id_type=MESH
        )
        return carry

    lax.fori_loop(1, n_dev, greet, 0)

    load_start = pltpu.make_async_copy(start_ref, vb.at[0], load_sem.at[0])
    load_k = pltpu.make_async_copy(k_ref, k_in, load_sem.at[1])
    load_mass = pltpu.make_async_copy(mass_hbm, mass_ref, load_sem.at[2])
    load_small = [
        pltpu.make_async_copy(source, target, load_sem.at[3 + i])
        for i, (source, target) in enumerate(
            ((panel_hbm, panel_ref), (low_hbm, low_ref), (high_hbm, high_ref), (cols_hbm, cols_ref))
        )
    ]
    for load in load_small:
        load.start()
    load_start.start()
    load_mass.start()
    load_k.start()
    for load in load_small:
        load.wait()

    def build_tables():
        def repeat(j, carry):
            named = lax.rem(j, n_col) * n_row + j // n_col
            spot = pl.ds(pl.multiple_of(j * slots, slots), slots)
            rep[spot, :] = jnp.broadcast_to(panel_ref[pl.ds(named, 1), :], (slots, per_block))
            return carry

        lax.fori_loop(0, n_dev, repeat, 0)
        cube = (n_dev, slots, per_block)
        slot_of = lax.broadcasted_iota(jnp.int32, cube, 1).reshape(flat, per_block)
        owner_of = lax.broadcasted_iota(jnp.int32, cube, 0).reshape(flat, per_block)
        lane = lax.broadcasted_iota(jnp.int32, (flat, per_block), 1)

        def hits(values, base):
            owned = (values >= base) & (values < base + rows)
            spot = jnp.where(owned, lane, per_block).astype(jnp.float32)
            first = jnp.min(spot, axis=1, keepdims=True).astype(jnp.int32)
            return owned & (lane - first == slot_of)

        values = rep[...]
        hit = hits(values, me * rows)
        local = jnp.where(hit, values - me * rows + 1, 0).astype(jnp.float32)
        local = jnp.sum(local, axis=1, keepdims=True) - 1.0
        across = jnp.broadcast_to(local, (flat, per_block)).T[0:1, :].astype(jnp.int32)
        down = local.astype(jnp.int32)
        one = jnp.ones((), jnp.float32)
        zero = jnp.zeros((), jnp.float32)
        wide = lax.broadcasted_iota(jnp.int32, (flat, rows), 1)
        pick[...] = jnp.where(wide == down, one, zero).astype(jnp.bfloat16)
        tall = lax.broadcasted_iota(jnp.int32, (rows, flat), 0)
        place[...] = jnp.where(tall == across, one, zero).astype(jnp.bfloat16)
        mine = jnp.broadcast_to(
            panel_ref[pl.ds(my_col * n_row + my_row, 1), :], (flat, per_block)
        )
        order = jnp.where(hits(mine, owner_of * rows), one, zero)
        order_out[...] = order.astype(jnp.bfloat16)
        order_in[...] = order.T.astype(jnp.bfloat16)

    lower = low_ref[...].astype(jnp.float32) * 0.25
    upper = high_ref[...].astype(jnp.float32) * 0.25
    centre[...] = 0.5 * (upper + lower)
    inverse[...] = 1.0 / (0.5 * (upper - lower))
    norm[...] = jnp.ones_like(norm)
    build_tables()
    pl.semaphore_wait(barrier, n_dev - 1)

    def remote(source, target, send, recv, to):
        return pltpu.make_async_remote_copy(
            src_ref=source, dst_ref=target, send_sem=send, recv_sem=recv,
            device_id=to, device_id_type=MESH,
        )

    def far(k):
        below = n_col - 1 - k
        below = jnp.where(below <= my_col, below - 1, below)
        above = jnp.where(k >= my_col, k + 1, k)
        return jnp.where(2 * my_col < n_col, below, above)

    def everyone(act):
        def line(k, first):
            row = lax.rem(my_row + k, n_row)
            for j in range(first, n_col):
                col = lax.rem(my_col + j, n_col)
                act(row * n_col + col, (row, col))

        def step(k, carry):
            line(k, 0)
            return carry

        lax.fori_loop(1, n_row, step, 0)
        line(0, 1)

    partner = my_row + 1 - 2 * lax.rem(my_row, 2)

    def wait_everyone(out, into, send, recv):
        others = pl.ds(0, n_dev - 1)
        remote(out.at[others], into.at[others], send, recv, (partner, my_col)).wait()

    def first_copy(to, where):
        return remote(first_out.at[to], first_in.at[me], first_send.at[0], first_recv.at[0], where)

    def coded_copies(out, out_s, into, into_s, send, recv, slot, to, where):
        return (
            remote(out.at[to], into.at[slot, me], send.at[0], recv.at[slot, 0], where),
            remote(out_s.at[to], into_s.at[slot, me], send.at[1], recv.at[slot, 1], where),
        )

    disp_copies = functools.partial(
        coded_copies, disp_out, disp_s, disp_in, disp_si, disp_send, disp_recv
    )
    ret_copies = functools.partial(
        coded_copies, ret_out, ret_s, ret_in, ret_si, ret_send, ret_recv
    )

    def exchange_start(copies, slot):
        def act(to, where):
            for copy in copies(slot, to, where):
                copy.start()

        everyone(act)

    def disp_wait(slot):
        wait_everyone(disp_out, disp_in.at[slot], disp_send.at[0], disp_recv.at[slot, 0])
        wait_everyone(disp_s, disp_si.at[slot], disp_send.at[1], disp_recv.at[slot, 1])

    def ret_wait(slot):
        wait_everyone(ret_out, ret_in.at[slot], ret_send.at[0], ret_recv.at[slot, 0])
        wait_everyone(ret_s, ret_si.at[slot], ret_send.at[1], ret_recv.at[slot, 1])

    def scatter_coded(value, out, out_s, into, into_s, copies, slot):
        cube = value.reshape(n_dev, slots, width)
        largest = jnp.maximum(jnp.max(jnp.abs(cube), axis=1, keepdims=True), 1e-30)
        scale = (largest * (MARGIN / LIMIT)).astype(jnp.bfloat16).astype(jnp.float32)
        out[...] = jnp.round(cube * (1.0 / scale)).astype(jnp.int32).astype(jnp.int16)
        pieces = [scale[:, :, : width // 2], scale[:, :, width // 2 :]]
        out_s[...] = jnp.concatenate(pieces, axis=1).astype(jnp.bfloat16)
        exchange_start(copies, slot)
        into[slot, me] = out[me]
        into_s[slot, me] = out_s[me]

    def collect(into, into_s, slot):
        pieces = into_s[slot].astype(jnp.float32)
        scale = jnp.concatenate([pieces[:, 0:1, :], pieces[:, 1:2, :]], axis=2)
        return split(decode(into[slot], scale).reshape(flat, width))

    chips = n_row // 2

    def wet_copy(k):
        to = (lax.rem(my_row + 2 * k, n_row), my_col)
        return remote(wet.at[my_row], wet.at[my_row], wet_send.at[k], wet_recv.at[k], to)

    def wet_forward(k):
        held = wet.at[lax.rem(my_row + n_row - 2 * k, n_row)]
        return remote(
            held, held, wet_send.at[chips + k], wet_recv.at[chips + k], (partner, my_col)
        )

    def gather_start():
        for k in range(1, chips):
            wet_copy(k).start()
        wet_forward(0).start()

    def gather_wait():
        for k in range(1, chips):
            wet_copy(k).wait_recv()
            wet_forward(k).start()
        for k in range(1, chips):
            wet_copy(k).wait_send()
        for k in range(chips):
            wet_forward(k).wait()

    def rs_copies(to):
        where = (my_row, to)
        return (
            remote(rs_out.at[to], rs_in.at[my_col], rs_send.at[0], rs_recv.at[0], where),
            remote(rs_s.at[to], rs_si.at[my_col], rs_send.at[1], rs_recv.at[1], where),
        )

    def product_start():
        gathered = wet[...].reshape(n_row * per_block, width)

        def product(index):
            chunk = pl.ds(pl.multiple_of(index * per_block, per_block), per_block)
            return dot(mass[chunk, :], gathered)

        for k in range(n_col - 1):
            other = far(k)
            coded, scale = encode(product(other), 0)
            rs_out[other] = coded
            rs_s[other] = scale
            for copy in rs_copies(other):
                copy.start()
        pressure[...] = product(my_col)

    def product_wait():
        others = pl.ds(0, n_col - 1)
        where = (partner, my_col)
        remote(rs_out.at[others], rs_in.at[others], rs_send.at[0], rs_recv.at[0], where).wait()
        remote(rs_s.at[others], rs_si.at[others], rs_send.at[1], rs_recv.at[1], where).wait()
        total = pressure[...]
        for k in range(1, n_col):
            other = lax.rem(my_col + k, n_col)
            total = total + decode(rs_in[other], rs_si[other])
        pressure[...] = total

    def halo_copies(side):
        where = device(lax.rem(me + 1 + side * (n_dev - 2), n_dev))
        return (
            remote(
                halo_out.at[side], halo_in.at[side], halo_send.at[0, side], halo_recv.at[0, side],
                where,
            ),
            remote(
                halo_s.at[side], halo_si.at[side], halo_send.at[1, side], halo_recv.at[1, side],
                where,
            ),
        )

    def halo_start(slot):
        lead = jnp.where(my_col == 0, 1, 0)
        for turn in range(2):
            side = lead if turn == 0 else 1 - lead
            spot = pl.multiple_of((1 - side) * (rows - pair), pair)
            coded, scale = encode(vb[slot, pl.ds(spot, pair), :], 0)
            halo_out[side] = coded
            halo_s[side] = scale
            for copy in halo_copies(side):
                copy.start()

    def banded(q, first, values_hi, values_lo):
        count = values_hi.shape[0]
        window_hi = k_hi[q, :, first : first + count]
        window_lo = k_lo[q, :, first : first + count]
        return (
            dot(window_hi, values_hi) + dot(window_lo, values_hi) + dot(window_hi, values_lo)
        )

    def build_band():
        for q in range(pairs):
            for half in range(2):
                i = 2 * q + half
                base = me * blocks - 2 + 2 * q
                for o in range(6):
                    total = jnp.zeros((block, block), jnp.float32)
                    for k in range(terms):
                        flag = (cols_ref[k, i] - base == o).astype(jnp.float32)
                        total = total + k_in[i, k] * flag
                    high, low = split(total)
                    k_hi[q, half * block : (half + 1) * block, o * block : (o + 1) * block] = high
                    k_lo[q, half * block : (half + 1) * block, o * block : (o + 1) * block] = low

    def inner_stiffness():
        for q in range(pairs):
            first = max(q - 1, 0) * pair
            last = min(q + 2, pairs) * pair
            stiff[q * pair : (q + 1) * pair, :] = banded(
                q, pair if q == 0 else 0, v_hi[first:last, :], v_lo[first:last, :]
            )

    def outer_stiffness():
        for side in range(2):
            for copy in halo_copies(side):
                copy.wait()
        high, low = split(decode(halo_in[0], halo_si[0]))
        stiff[0:pair, :] += banded(0, 0, high, low)
        high, low = split(decode(halo_in[1], halo_si[1]))
        stiff[rows - pair : rows, :] += banded(pairs - 1, 2 * pair, high, low)

    def alpha(step):
        start = lax.rem(step, DEGREE) == 0
        factor = jnp.where(start, 1.0, 2.0).astype(jnp.float32)
        scaled = start & (step > 0)
        return inverse[...] * factor * jnp.where(scaled, norm[...], 1.0)

    def beta(step):
        place_in = lax.rem(step, DEGREE)
        factor = jnp.where(place_in == 0, 0.0, 1.0).astype(jnp.float32)
        scaled = (place_in == 1) & (step > 1)
        return factor * jnp.where(scaled, norm[...], 1.0)

    def known_part(step, slot, first, last):
        mine = alpha(step) * (stiff[first:last, :] - centre[...] * vb[slot, first:last, :])
        mine = mine - beta(step) * vb[1 - slot, first:last, :]
        stiff[first:last, :] = mine
        high, low = split(mine)
        return dot(pick[:, first:last], high) + dot(pick[:, first:last], low)

    def known_inner(step, slot):
        chosen_part[...] = known_part(step, slot, pair, rows - pair)

    def send_known(step, slot):
        chosen = chosen_part[...] + known_part(step, slot, 0, pair)
        chosen = chosen + known_part(step, slot, rows - pair, rows)
        scatter_coded(
            chosen, disp_out, disp_s, disp_in, disp_si, disp_copies, lax.rem(step, 2)
        )

    def send_pressure(slot):
        high, low = split(pressure[...])
        ordered = dot(order_out[...], high) + dot(order_out[...], low)
        scatter_coded(ordered, ret_out, ret_s, ret_in, ret_si, ret_copies, slot)

    def next_values(step, slot, edges):
        parity = lax.rem(step, 2)
        ret_wait(parity)
        high, low = collect(ret_in, ret_si, parity)

        def update(first, last):
            loads = dot(place[first:last, :], high) + dot(place[first:last, :], low)
            vb[1 - slot, first:last, :] = stiff[first:last, :] + alpha(step) * loads

        update(0, pair)
        update(rows - pair, rows)
        if edges:
            halo_start(1 - slot)
        update(pair, rows - pair)

    def square_start(outer, panels):
        shells = stiff[...] * dry[...]
        sq_out[...] = jnp.sum(shells * shells, axis=0, keepdims=True) + jnp.sum(
            panels * panels, axis=0, keepdims=True
        )

        def act(to, where):
            remote(sq_out, sq_in.at[outer, me], sq_send.at[outer], sq_recv.at[outer], where).start()

        everyone(act)
        sq_in[outer, me] = sq_out[...]

    def square_wait(outer):
        arrived = sq_in.at[outer]
        wait_everyone(arrived, arrived, sq_send.at[outer], sq_recv.at[outer])
        squares = jnp.sum(sq_in[outer], axis=0)
        return 1.0 / jnp.sqrt(squares / (rows * n_dev) + 1e-06)

    def panel_values(step):
        slot = lax.rem(step, 2)
        disp_wait(slot)
        high, low = collect(disp_in, disp_si, slot)
        known = dot(order_in[...], high) + dot(order_in[...], low)
        return known + alpha(step) * pressure[...]

    def split_values(slot):
        high, low = split(vb[slot])
        v_hi[...] = high
        v_lo[...] = low

    def mass_place(i):
        index = n_col * my_row + i
        to = lax.rem(index, n_row)
        source = mass_ref.at[pl.ds(i * per_block, per_block), :]
        spot = pl.multiple_of((index // n_row) * per_block, per_block)
        return to, source, mass.at[pl.ds(spot, per_block), :], index // n_row

    def mass_start(wave):
        for i in range(wave, n_col, 2):
            to, source, target, spot = mass_place(i)

            @pl.when(to != my_row)
            def _():
                remote(source, target, mass_send.at[i], mass_recv.at[spot], (to, my_col)).start()

            @pl.when(to == my_row)
            def _():
                pltpu.make_async_copy(source, target, mass_send.at[i]).start()

    def mass_wait():
        for i in range(n_col):
            to, source, target, spot = mass_place(i)

            @pl.when(to != my_row)
            def _():
                remote(
                    source, target, mass_send.at[i], mass_recv.at[spot], (to, my_col)
                ).wait_send()

            @pl.when(to == my_row)
            def _():
                pltpu.make_async_copy(source, target, mass_send.at[i]).wait()

        for q in range(n_col):
            index = q * n_row + my_row
            target = mass.at[pl.ds(q * per_block, per_block), :]
            source = mass_ref.at[pl.ds(0, per_block), :]

            @pl.when(index // n_col != my_row)
            def _():
                remote(
                    source, target, mass_send.at[q], mass_recv.at[q], (index // n_col, my_col)
                ).wait_recv()

    load_start.wait()
    split_values(0)
    first_out[...] = dot(pick[...], v_hi[...]).reshape(n_dev, slots, width).astype(jnp.bfloat16)
    everyone(lambda to, where: first_copy(to, where).start())
    first_in[me] = first_out[me]
    halo_start(0)
    load_mass.wait()
    mass_start(0)
    load_k.wait()
    build_band()
    inner_stiffness()
    ones = jnp.ones((flat, width), jnp.bfloat16)
    dry[...] = 1.0 - dot(place[...], ones)
    wait_everyone(first_out, first_in, first_send.at[0], first_recv.at[0])
    arrived = first_in[...].astype(jnp.float32).reshape(flat, width).astype(jnp.bfloat16)
    wet[my_row] = dot(order_in[...], arrived).astype(jnp.bfloat16)
    gather_start()
    mass_start(1)
    outer_stiffness()
    gather_wait()
    mass_wait()
    product_start()
    known_inner(0, 0)
    send_known(0, 0)
    product_wait()

    def step_of(step, carry):
        slot = lax.rem(step, 2)
        ends = lax.rem(step, DEGREE) == DEGREE - 1
        outer = step // DEGREE
        send_pressure(slot)
        panels = panel_values(step)
        wet[my_row] = panels.astype(jnp.bfloat16)
        gather_start()

        @pl.when(ends)
        def _():
            square_start(outer, panels)

        next_values(step, slot, True)
        split_values(1 - slot)
        gather_wait()
        product_start()
        inner_stiffness()

        @pl.when(ends)
        def _():
            norm[...] = square_wait(outer)

        known_inner(step + 1, 1 - slot)
        outer_stiffness()
        send_known(step + 1, 1 - slot)
        product_wait()
        return carry

    lax.fori_loop(0, STEPS - 1, step_of, 0)
    last = STEPS - 1
    slot = last % 2
    send_pressure(slot)
    square_start(OUTER - 1, panel_values(last))
    next_values(last, slot, False)
    store = pltpu.make_async_copy(vb.at[1 - slot], result_ref, load_sem.at[0])
    store.start()
    scale_ref[...] = square_wait(OUTER - 1)
    store.wait()


def body(mode_block, k_blocks, block_cols, panel_node, added_mass, low_edge, high_edge):
    n_row = lax.axis_size("row")
    n_col = lax.axis_size("col")
    devices = n_row * n_col
    rows_dev, width = mode_block.shape
    block_size = k_blocks.shape[2]
    per_block = panel_node.shape[0] // devices
    most = 2 * ((per_block + devices - 1) // devices)
    slots = (most + SUBLANES - 1) // SUBLANES * SUBLANES
    flat = devices * slots
    pair = 2 * block_size
    pairs = rows_dev // pair
    f32, bf16, i16 = jnp.float32, jnp.bfloat16, jnp.int16
    vmem = pl.BlockSpec(memory_space=pltpu.VMEM)
    anywhere = pl.BlockSpec(memory_space=pl.ANY)
    dma = pltpu.SemaphoreType.DMA
    coded = pltpu.VMEM((devices, slots, width), i16)
    coded_in = pltpu.VMEM((2, devices, slots, width), i16)
    scale = pltpu.VMEM((devices, 2, width // 2), bf16)
    scale_in = pltpu.VMEM((2, devices, 2, width // 2), bf16)
    row = pltpu.VMEM((1, width), f32)
    values, factor = pl.pallas_call(
        functools.partial(kernel, n_row, n_col),
        out_shape=(
            jax.ShapeDtypeStruct(mode_block.shape, f32),
            jax.ShapeDtypeStruct((1, width), f32),
        ),
        in_specs=[anywhere] * 7,
        out_specs=(anywhere, vmem),
        scratch_shapes=[
            pltpu.SMEM(block_cols.shape[::-1], jnp.int32),
            pltpu.VMEM((devices, per_block), jnp.int32),
            pltpu.VMEM((1, width), jnp.int32),
            pltpu.VMEM((1, width), jnp.int32),
            pltpu.VMEM(added_mass.shape, bf16),
            pltpu.VMEM((2, rows_dev, width), f32),
            pltpu.VMEM((rows_dev, width), bf16),
            pltpu.VMEM((rows_dev, width), bf16),
            pltpu.VMEM((rows_dev, width), f32),
            pltpu.VMEM(k_blocks.shape, f32),
            pltpu.VMEM((pairs, pair, 3 * pair), bf16),
            pltpu.VMEM((pairs, pair, 3 * pair), bf16),
            pltpu.VMEM(added_mass.shape, bf16),
            pltpu.VMEM((flat, per_block), jnp.int32),
            pltpu.VMEM((flat, rows_dev), bf16),
            pltpu.VMEM((rows_dev, flat), bf16),
            pltpu.VMEM((per_block, flat), bf16),
            pltpu.VMEM((flat, per_block), bf16),
            pltpu.VMEM((devices, slots, width), bf16),
            pltpu.VMEM((devices, slots, width), bf16),
            coded, coded_in, scale, scale_in,
            pltpu.VMEM((n_row, per_block, width), bf16),
            pltpu.VMEM((n_col, per_block, width), i16),
            pltpu.VMEM((n_col, per_block, width), i16),
            pltpu.VMEM((n_col, 1, width), f32),
            pltpu.VMEM((n_col, 1, width), f32),
            pltpu.VMEM((per_block, width), f32),
            coded, coded_in, scale, scale_in,
            pltpu.VMEM((2, pair, width), i16),
            pltpu.VMEM((2, pair, width), i16),
            pltpu.VMEM((2, 1, width), f32),
            pltpu.VMEM((2, 1, width), f32),
            row, row, row, row,
            pltpu.VMEM((OUTER, devices, 1, width), f32),
            pltpu.VMEM((rows_dev, width), f32),
            pltpu.VMEM((flat, width), f32),
            dma((7,)),
            dma((n_col,)),
            dma((n_col,)),
            dma((1,)),
            dma((1,)),
            dma((2,)),
            dma((2, 2)),
            dma((n_row,)),
            dma((n_row,)),
            dma((2,)),
            dma((2,)),
            dma((2,)),
            dma((2, 2)),
            dma((2, 2)),
            dma((2, 2)),
            dma((OUTER,)),
            dma((OUTER,)),
        ],
        compiler_params=pltpu.CompilerParams(
            collective_id=0, has_side_effects=True, vmem_limit_bytes=60 * 1024 * 1024
        ),
    )(
        block_cols.T,
        panel_node.reshape(devices, per_block),
        low_edge.reshape(1, width),
        high_edge.reshape(1, width),
        mode_block,
        k_blocks,
        added_mass,
    )
    return values * factor


def solution(mesh):
    placed = (
        P(("row", "col"), None),
        P(("row", "col"), None, None, None),
        P(("row", "col"), None),
        P(),
        P("row", "col"),
        P(),
        P(),
    )
    return jax.shard_map(
        body, mesh=mesh, in_specs=placed, out_specs=P(("row", "col"), None), check_vma=False
    )
```

```python
import functools

import jax
import jax.numpy as jnp
from jax import lax
from jax.experimental import pallas as pl
from jax.experimental.pallas import tpu as pltpu
from jax.sharding import PartitionSpec as P

DEGREE = 3
OUTER = 2
STEPS = DEGREE * OUTER
SUBLANES = 8
LIMIT = 32767.0
MARGIN = 1.004
MESH = pl.DeviceIdType.MESH


def dot(left, right):
    return jnp.dot(left, right, preferred_element_type=jnp.float32)


def split(value):
    high = value.astype(jnp.bfloat16)
    low = (value - high.astype(jnp.float32)).astype(jnp.bfloat16)
    return high, low


def encode(value, axis):
    largest = jnp.maximum(jnp.max(jnp.abs(value), axis=axis, keepdims=True), 1e-30)
    coded = jnp.round(value * (LIMIT / largest))
    return coded.astype(jnp.int32).astype(jnp.int16), largest * (1.0 / LIMIT)


def decode(coded, scale):
    return coded.astype(jnp.int32).astype(jnp.float32) * scale


def kernel(
    n_row, n_col,
    cols_hbm, panel_hbm, low_hbm, high_hbm, start_ref, k_ref, mass_hbm,
    result_ref, scale_ref,
    cols_ref, panel_ref, low_ref, high_ref, mass_ref, vb, v_hi, v_lo, stiff, k_in, k_hi, k_lo, mass, rep, pick, place, order_in, order_out,
    first_out, first_in, disp_out, disp_in, disp_s, disp_si, wet,
    rs_out, rs_in, rs_s, rs_si, pressure,
    ret_out, ret_in, ret_s, ret_si, halo_out, halo_in, halo_s, halo_si,
    centre, inverse, norm, sq_out, sq_in, dry, chosen_part,
    load_sem, mass_send, mass_recv, first_send, first_recv, disp_send, disp_recv, wet_send, wet_recv,
    rs_send, rs_recv, ret_send, ret_recv, halo_send, halo_recv, sq_send, sq_recv,
):
    n_dev = n_row * n_col
    my_row = lax.axis_index("row")
    my_col = lax.axis_index("col")
    me = my_row * n_col + my_col
    rows, width = v_hi.shape
    slots = disp_out.shape[1]
    flat = n_dev * slots
    blocks, terms, block = k_in.shape[0], k_in.shape[1], k_in.shape[2]
    pair = 2 * block
    pairs = rows // pair
    per_block = order_in.shape[0]

    def device(index):
        return (index // n_col, lax.rem(index, n_col))

    barrier = pltpu.get_barrier_semaphore()

    def greet(k, carry):
        pl.semaphore_signal(
            barrier, inc=1, device_id=device(lax.rem(me + k, n_dev)), device_id_type=MESH
        )
        return carry

    lax.fori_loop(1, n_dev, greet, 0)

    load_start = pltpu.make_async_copy(start_ref, vb.at[0], load_sem.at[0])
    load_k = pltpu.make_async_copy(k_ref, k_in, load_sem.at[1])
    load_mass = pltpu.make_async_copy(mass_hbm, mass_ref, load_sem.at[2])
    load_small = [
        pltpu.make_async_copy(source, target, load_sem.at[3 + i])
        for i, (source, target) in enumerate(
            ((panel_hbm, panel_ref), (low_hbm, low_ref), (high_hbm, high_ref), (cols_hbm, cols_ref))
        )
    ]
    for load in load_small:
        load.start()
    load_start.start()
    load_mass.start()
    load_k.start()
    for load in load_small:
        load.wait()

    def build_tables():
        def repeat(j, carry):
            named = lax.rem(j, n_col) * n_row + j // n_col
            spot = pl.ds(pl.multiple_of(j * slots, slots), slots)
            rep[spot, :] = jnp.broadcast_to(panel_ref[pl.ds(named, 1), :], (slots, per_block))
            return carry

        lax.fori_loop(0, n_dev, repeat, 0)
        cube = (n_dev, slots, per_block)
        slot_of = lax.broadcasted_iota(jnp.int32, cube, 1).reshape(flat, per_block)
        owner_of = lax.broadcasted_iota(jnp.int32, cube, 0).reshape(flat, per_block)
        lane = lax.broadcasted_iota(jnp.int32, (flat, per_block), 1)

        def hits(values, base):
            owned = (values >= base) & (values < base + rows)
            spot = jnp.where(owned, lane, per_block).astype(jnp.float32)
            first = jnp.min(spot, axis=1, keepdims=True).astype(jnp.int32)
            return owned & (lane - first == slot_of)

        values = rep[...]
        hit = hits(values, me * rows)
        local = jnp.where(hit, values - me * rows + 1, 0).astype(jnp.float32)
        local = jnp.sum(local, axis=1, keepdims=True) - 1.0
        across = jnp.broadcast_to(local, (flat, per_block)).T[0:1, :].astype(jnp.int32)
        down = local.astype(jnp.int32)
        one = jnp.ones((), jnp.float32)
        zero = jnp.zeros((), jnp.float32)
        wide = lax.broadcasted_iota(jnp.int32, (flat, rows), 1)
        pick[...] = jnp.where(wide == down, one, zero).astype(jnp.bfloat16)
        tall = lax.broadcasted_iota(jnp.int32, (rows, flat), 0)
        place[...] = jnp.where(tall == across, one, zero).astype(jnp.bfloat16)
        mine = jnp.broadcast_to(
            panel_ref[pl.ds(my_col * n_row + my_row, 1), :], (flat, per_block)
        )
        order = jnp.where(hits(mine, owner_of * rows), one, zero)
        order_out[...] = order.astype(jnp.bfloat16)
        order_in[...] = order.T.astype(jnp.bfloat16)

    lower = low_ref[...].astype(jnp.float32) * 0.25
    upper = high_ref[...].astype(jnp.float32) * 0.25
    centre[...] = 0.5 * (upper + lower)
    inverse[...] = 1.0 / (0.5 * (upper - lower))
    norm[...] = jnp.ones_like(norm)
    build_tables()
    pl.semaphore_wait(barrier, n_dev - 1)

    def remote(source, target, send, recv, to):
        return pltpu.make_async_remote_copy(
            src_ref=source, dst_ref=target, send_sem=send, recv_sem=recv,
            device_id=to, device_id_type=MESH,
        )

    def far(k):
        below = n_col - 1 - k
        below = jnp.where(below <= my_col, below - 1, below)
        above = jnp.where(k >= my_col, k + 1, k)
        return jnp.where(2 * my_col < n_col, below, above)

    def everyone(act):
        def line(k, first):
            row = lax.rem(my_row + k, n_row)
            for j in range(n_col - 1):
                col = far(j)
                act(row * n_col + col, (row, col))
            if first == 0:
                act(row * n_col + my_col, (row, my_col))

        def step(k, carry):
            line(k, 0)
            return carry

        lax.fori_loop(1, n_row, step, 0)
        line(0, 1)

    partner = my_row + 1 - 2 * lax.rem(my_row, 2)

    def wait_everyone(out, into, send, recv):
        others = pl.ds(0, n_dev - 1)
        remote(out.at[others], into.at[others], send, recv, (partner, my_col)).wait()

    def first_copy(to, where):
        return remote(first_out.at[to], first_in.at[me], first_send.at[0], first_recv.at[0], where)

    def coded_copies(out, out_s, into, into_s, send, recv, slot, to, where):
        return (
            remote(out.at[to], into.at[slot, me], send.at[0], recv.at[slot, 0], where),
            remote(out_s.at[to], into_s.at[slot, me], send.at[1], recv.at[slot, 1], where),
        )

    disp_copies = functools.partial(
        coded_copies, disp_out, disp_s, disp_in, disp_si, disp_send, disp_recv
    )
    ret_copies = functools.partial(
        coded_copies, ret_out, ret_s, ret_in, ret_si, ret_send, ret_recv
    )

    def exchange_start(copies, slot):
        def act(to, where):
            for copy in copies(slot, to, where):
                copy.start()

        everyone(act)

    def disp_wait(slot):
        wait_everyone(disp_out, disp_in.at[slot], disp_send.at[0], disp_recv.at[slot, 0])
        wait_everyone(disp_s, disp_si.at[slot], disp_send.at[1], disp_recv.at[slot, 1])

    def ret_wait(slot):
        wait_everyone(ret_out, ret_in.at[slot], ret_send.at[0], ret_recv.at[slot, 0])
        wait_everyone(ret_s, ret_si.at[slot], ret_send.at[1], ret_recv.at[slot, 1])

    def scatter_coded(value, out, out_s, into, into_s, copies, slot):
        cube = value.reshape(n_dev, slots, width)
        largest = jnp.maximum(jnp.max(jnp.abs(cube), axis=1, keepdims=True), 1e-30)
        scale = (largest * (MARGIN / LIMIT)).astype(jnp.bfloat16).astype(jnp.float32)
        out[...] = jnp.round(cube * (1.0 / scale)).astype(jnp.int32).astype(jnp.int16)
        pieces = [scale[:, :, : width // 2], scale[:, :, width // 2 :]]
        out_s[...] = jnp.concatenate(pieces, axis=1).astype(jnp.bfloat16)
        exchange_start(copies, slot)
        into[slot, me] = out[me]
        into_s[slot, me] = out_s[me]

    def collect(into, into_s, slot):
        pieces = into_s[slot].astype(jnp.float32)
        scale = jnp.concatenate([pieces[:, 0:1, :], pieces[:, 1:2, :]], axis=2)
        return split(decode(into[slot], scale).reshape(flat, width))

    chips = n_row // 2

    def wet_copy(k):
        to = (lax.rem(my_row + 2 * k, n_row), my_col)
        return remote(wet.at[my_row], wet.at[my_row], wet_send.at[k], wet_recv.at[k], to)

    def wet_forward(k):
        held = wet.at[lax.rem(my_row + n_row - 2 * k, n_row)]
        return remote(
            held, held, wet_send.at[chips + k], wet_recv.at[chips + k], (partner, my_col)
        )

    def gather_start():
        for k in range(1, chips):
            wet_copy(k).start()
        wet_forward(0).start()

    def gather_wait():
        for k in range(1, chips):
            wet_copy(k).wait_recv()
            wet_forward(k).start()
        for k in range(1, chips):
            wet_copy(k).wait_send()
        for k in range(chips):
            wet_forward(k).wait()

    def rs_copies(to):
        where = (my_row, to)
        return (
            remote(rs_out.at[to], rs_in.at[my_col], rs_send.at[0], rs_recv.at[0], where),
            remote(rs_s.at[to], rs_si.at[my_col], rs_send.at[1], rs_recv.at[1], where),
        )

    def product_start():
        gathered = wet[...].reshape(n_row * per_block, width)

        def product(index):
            chunk = pl.ds(pl.multiple_of(index * per_block, per_block), per_block)
            return dot(mass[chunk, :], gathered)

        for k in range(n_col - 1):
            other = far(k)
            coded, scale = encode(product(other), 0)
            rs_out[other] = coded
            rs_s[other] = scale
            for copy in rs_copies(other):
                copy.start()
        pressure[...] = product(my_col)

    def product_wait():
        others = pl.ds(0, n_col - 1)
        where = (partner, my_col)
        remote(rs_out.at[others], rs_in.at[others], rs_send.at[0], rs_recv.at[0], where).wait()
        remote(rs_s.at[others], rs_si.at[others], rs_send.at[1], rs_recv.at[1], where).wait()
        total = pressure[...]
        for k in range(1, n_col):
            other = lax.rem(my_col + k, n_col)
            total = total + decode(rs_in[other], rs_si[other])
        pressure[...] = total

    def halo_copies(side):
        where = device(lax.rem(me + 1 + side * (n_dev - 2), n_dev))
        return (
            remote(
                halo_out.at[side], halo_in.at[side], halo_send.at[0, side], halo_recv.at[0, side],
                where,
            ),
            remote(
                halo_s.at[side], halo_si.at[side], halo_send.at[1, side], halo_recv.at[1, side],
                where,
            ),
        )

    def halo_start(slot):
        lead = jnp.where(my_col == 0, 1, 0)
        for turn in range(2):
            side = lead if turn == 0 else 1 - lead
            spot = pl.multiple_of((1 - side) * (rows - pair), pair)
            coded, scale = encode(vb[slot, pl.ds(spot, pair), :], 0)
            halo_out[side] = coded
            halo_s[side] = scale
            for copy in halo_copies(side):
                copy.start()

    def banded(q, first, values_hi, values_lo):
        count = values_hi.shape[0]
        window_hi = k_hi[q, :, first : first + count]
        window_lo = k_lo[q, :, first : first + count]
        return (
            dot(window_hi, values_hi) + dot(window_lo, values_hi) + dot(window_hi, values_lo)
        )

    def build_band():
        for q in range(pairs):
            for half in range(2):
                i = 2 * q + half
                base = me * blocks - 2 + 2 * q
                for o in range(6):
                    total = jnp.zeros((block, block), jnp.float32)
                    for k in range(terms):
                        flag = (cols_ref[k, i] - base == o).astype(jnp.float32)
                        total = total + k_in[i, k] * flag
                    high, low = split(total)
                    k_hi[q, half * block : (half + 1) * block, o * block : (o + 1) * block] = high
                    k_lo[q, half * block : (half + 1) * block, o * block : (o + 1) * block] = low

    def inner_stiffness():
        for q in range(pairs):
            first = max(q - 1, 0) * pair
            last = min(q + 2, pairs) * pair
            stiff[q * pair : (q + 1) * pair, :] = banded(
                q, pair if q == 0 else 0, v_hi[first:last, :], v_lo[first:last, :]
            )

    def outer_stiffness():
        for side in range(2):
            for copy in halo_copies(side):
                copy.wait()
        high, low = split(decode(halo_in[0], halo_si[0]))
        stiff[0:pair, :] += banded(0, 0, high, low)
        high, low = split(decode(halo_in[1], halo_si[1]))
        stiff[rows - pair : rows, :] += banded(pairs - 1, 2 * pair, high, low)

    def alpha(step):
        start = lax.rem(step, DEGREE) == 0
        factor = jnp.where(start, 1.0, 2.0).astype(jnp.float32)
        scaled = start & (step > 0)
        return inverse[...] * factor * jnp.where(scaled, norm[...], 1.0)

    def beta(step):
        place_in = lax.rem(step, DEGREE)
        factor = jnp.where(place_in == 0, 0.0, 1.0).astype(jnp.float32)
        scaled = (place_in == 1) & (step > 1)
        return factor * jnp.where(scaled, norm[...], 1.0)

    def known_part(step, slot, first, last):
        mine = alpha(step) * (stiff[first:last, :] - centre[...] * vb[slot, first:last, :])
        mine = mine - beta(step) * vb[1 - slot, first:last, :]
        stiff[first:last, :] = mine
        high, low = split(mine)
        return dot(pick[:, first:last], high) + dot(pick[:, first:last], low)

    def known_inner(step, slot):
        chosen_part[...] = known_part(step, slot, pair, rows - pair)

    def send_known(step, slot):
        chosen = chosen_part[...] + known_part(step, slot, 0, pair)
        chosen = chosen + known_part(step, slot, rows - pair, rows)
        scatter_coded(
            chosen, disp_out, disp_s, disp_in, disp_si, disp_copies, lax.rem(step, 2)
        )

    def send_pressure(slot):
        high, low = split(pressure[...])
        ordered = dot(order_out[...], high) + dot(order_out[...], low)
        scatter_coded(ordered, ret_out, ret_s, ret_in, ret_si, ret_copies, slot)

    def next_values(step, slot, edges):
        parity = lax.rem(step, 2)
        ret_wait(parity)
        high, low = collect(ret_in, ret_si, parity)

        def update(first, last):
            loads = dot(place[first:last, :], high) + dot(place[first:last, :], low)
            vb[1 - slot, first:last, :] = stiff[first:last, :] + alpha(step) * loads

        update(0, pair)
        update(rows - pair, rows)
        if edges:
            halo_start(1 - slot)
        update(pair, rows - pair)

    def square_start(outer, panels):
        shells = stiff[...] * dry[...]
        sq_out[...] = jnp.sum(shells * shells, axis=0, keepdims=True) + jnp.sum(
            panels * panels, axis=0, keepdims=True
        )

        def act(to, where):
            remote(sq_out, sq_in.at[outer, me], sq_send.at[outer], sq_recv.at[outer], where).start()

        everyone(act)
        sq_in[outer, me] = sq_out[...]

    def square_wait(outer):
        arrived = sq_in.at[outer]
        wait_everyone(arrived, arrived, sq_send.at[outer], sq_recv.at[outer])
        squares = jnp.sum(sq_in[outer], axis=0)
        return 1.0 / jnp.sqrt(squares / (rows * n_dev) + 1e-06)

    def panel_values(step):
        slot = lax.rem(step, 2)
        disp_wait(slot)
        high, low = collect(disp_in, disp_si, slot)
        known = dot(order_in[...], high) + dot(order_in[...], low)
        return known + alpha(step) * pressure[...]

    def split_values(slot):
        high, low = split(vb[slot])
        v_hi[...] = high
        v_lo[...] = low

    def mass_place(i):
        index = n_col * my_row + i
        to = lax.rem(index, n_row)
        source = mass_ref.at[pl.ds(i * per_block, per_block), :]
        spot = pl.multiple_of((index // n_row) * per_block, per_block)
        return to, source, mass.at[pl.ds(spot, per_block), :], index // n_row

    def mass_start(wave):
        for i in range(wave, n_col, 2):
            to, source, target, spot = mass_place(i)

            @pl.when(to != my_row)
            def _():
                remote(source, target, mass_send.at[i], mass_recv.at[spot], (to, my_col)).start()

            @pl.when(to == my_row)
            def _():
                pltpu.make_async_copy(source, target, mass_send.at[i]).start()

    def mass_wait():
        for i in range(n_col):
            to, source, target, spot = mass_place(i)

            @pl.when(to != my_row)
            def _():
                remote(
                    source, target, mass_send.at[i], mass_recv.at[spot], (to, my_col)
                ).wait_send()

            @pl.when(to == my_row)
            def _():
                pltpu.make_async_copy(source, target, mass_send.at[i]).wait()

        for q in range(n_col):
            index = q * n_row + my_row
            target = mass.at[pl.ds(q * per_block, per_block), :]
            source = mass_ref.at[pl.ds(0, per_block), :]

            @pl.when(index // n_col != my_row)
            def _():
                remote(
                    source, target, mass_send.at[q], mass_recv.at[q], (index // n_col, my_col)
                ).wait_recv()

    load_start.wait()
    split_values(0)
    first_out[...] = dot(pick[...], v_hi[...]).reshape(n_dev, slots, width).astype(jnp.bfloat16)
    everyone(lambda to, where: first_copy(to, where).start())
    first_in[me] = first_out[me]
    halo_start(0)
    load_mass.wait()
    mass_start(0)
    load_k.wait()
    build_band()
    inner_stiffness()
    ones = jnp.ones((flat, width), jnp.bfloat16)
    dry[...] = 1.0 - dot(place[...], ones)
    wait_everyone(first_out, first_in, first_send.at[0], first_recv.at[0])
    arrived = first_in[...].astype(jnp.float32).reshape(flat, width).astype(jnp.bfloat16)
    wet[my_row] = dot(order_in[...], arrived).astype(jnp.bfloat16)
    gather_start()
    mass_start(1)
    outer_stiffness()
    gather_wait()
    mass_wait()
    product_start()
    known_inner(0, 0)
    send_known(0, 0)
    product_wait()

    def step_of(step, carry):
        slot = lax.rem(step, 2)
        ends = lax.rem(step, DEGREE) == DEGREE - 1
        outer = step // DEGREE
        send_pressure(slot)
        panels = panel_values(step)
        wet[my_row] = panels.astype(jnp.bfloat16)
        gather_start()

        @pl.when(ends)
        def _():
            square_start(outer, panels)

        next_values(step, slot, True)
        split_values(1 - slot)
        gather_wait()
        product_start()
        inner_stiffness()

        @pl.when(ends)
        def _():
            norm[...] = square_wait(outer)

        known_inner(step + 1, 1 - slot)
        outer_stiffness()
        send_known(step + 1, 1 - slot)
        product_wait()
        return carry

    lax.fori_loop(0, STEPS - 1, step_of, 0)
    last = STEPS - 1
    slot = last % 2
    send_pressure(slot)
    square_start(OUTER - 1, panel_values(last))
    next_values(last, slot, False)
    store = pltpu.make_async_copy(vb.at[1 - slot], result_ref, load_sem.at[0])
    store.start()
    scale_ref[...] = square_wait(OUTER - 1)
    store.wait()


def body(mode_block, k_blocks, block_cols, panel_node, added_mass, low_edge, high_edge):
    n_row = lax.axis_size("row")
    n_col = lax.axis_size("col")
    devices = n_row * n_col
    rows_dev, width = mode_block.shape
    block_size = k_blocks.shape[2]
    per_block = panel_node.shape[0] // devices
    most = 2 * ((per_block + devices - 1) // devices)
    slots = (most + SUBLANES - 1) // SUBLANES * SUBLANES
    flat = devices * slots
    pair = 2 * block_size
    pairs = rows_dev // pair
    f32, bf16, i16 = jnp.float32, jnp.bfloat16, jnp.int16
    vmem = pl.BlockSpec(memory_space=pltpu.VMEM)
    anywhere = pl.BlockSpec(memory_space=pl.ANY)
    dma = pltpu.SemaphoreType.DMA
    coded = pltpu.VMEM((devices, slots, width), i16)
    coded_in = pltpu.VMEM((2, devices, slots, width), i16)
    scale = pltpu.VMEM((devices, 2, width // 2), bf16)
    scale_in = pltpu.VMEM((2, devices, 2, width // 2), bf16)
    row = pltpu.VMEM((1, width), f32)
    values, factor = pl.pallas_call(
        functools.partial(kernel, n_row, n_col),
        out_shape=(
            jax.ShapeDtypeStruct(mode_block.shape, f32),
            jax.ShapeDtypeStruct((1, width), f32),
        ),
        in_specs=[anywhere] * 7,
        out_specs=(anywhere, vmem),
        scratch_shapes=[
            pltpu.SMEM(block_cols.shape[::-1], jnp.int32),
            pltpu.VMEM((devices, per_block), jnp.int32),
            pltpu.VMEM((1, width), jnp.int32),
            pltpu.VMEM((1, width), jnp.int32),
            pltpu.VMEM(added_mass.shape, bf16),
            pltpu.VMEM((2, rows_dev, width), f32),
            pltpu.VMEM((rows_dev, width), bf16),
            pltpu.VMEM((rows_dev, width), bf16),
            pltpu.VMEM((rows_dev, width), f32),
            pltpu.VMEM(k_blocks.shape, f32),
            pltpu.VMEM((pairs, pair, 3 * pair), bf16),
            pltpu.VMEM((pairs, pair, 3 * pair), bf16),
            pltpu.VMEM(added_mass.shape, bf16),
            pltpu.VMEM((flat, per_block), jnp.int32),
            pltpu.VMEM((flat, rows_dev), bf16),
            pltpu.VMEM((rows_dev, flat), bf16),
            pltpu.VMEM((per_block, flat), bf16),
            pltpu.VMEM((flat, per_block), bf16),
            pltpu.VMEM((devices, slots, width), bf16),
            pltpu.VMEM((devices, slots, width), bf16),
            coded, coded_in, scale, scale_in,
            pltpu.VMEM((n_row, per_block, width), bf16),
            pltpu.VMEM((n_col, per_block, width), i16),
            pltpu.VMEM((n_col, per_block, width), i16),
            pltpu.VMEM((n_col, 1, width), f32),
            pltpu.VMEM((n_col, 1, width), f32),
            pltpu.VMEM((per_block, width), f32),
            coded, coded_in, scale, scale_in,
            pltpu.VMEM((2, pair, width), i16),
            pltpu.VMEM((2, pair, width), i16),
            pltpu.VMEM((2, 1, width), f32),
            pltpu.VMEM((2, 1, width), f32),
            row, row, row, row,
            pltpu.VMEM((OUTER, devices, 1, width), f32),
            pltpu.VMEM((rows_dev, width), f32),
            pltpu.VMEM((flat, width), f32),
            dma((7,)),
            dma((n_col,)),
            dma((n_col,)),
            dma((1,)),
            dma((1,)),
            dma((2,)),
            dma((2, 2)),
            dma((n_row,)),
            dma((n_row,)),
            dma((2,)),
            dma((2,)),
            dma((2,)),
            dma((2, 2)),
            dma((2, 2)),
            dma((2, 2)),
            dma((OUTER,)),
            dma((OUTER,)),
        ],
        compiler_params=pltpu.CompilerParams(
            collective_id=0, has_side_effects=True, vmem_limit_bytes=60 * 1024 * 1024
        ),
    )(
        block_cols.T,
        panel_node.reshape(devices, per_block),
        low_edge.reshape(1, width),
        high_edge.reshape(1, width),
        mode_block,
        k_blocks,
        added_mass,
    )
    return values * factor


def solution(mesh):
    placed = (
        P(("row", "col"), None),
        P(("row", "col"), None, None, None),
        P(("row", "col"), None),
        P(),
        P("row", "col"),
        P(),
        P(),
    )
    return jax.shard_map(
        body, mesh=mesh, in_specs=placed, out_specs=P(("row", "col"), None), check_vma=False
    )
```
